128 devices in a mesh: leaf: 128 (over x, z, y, core).
Axes of the slice: x: 4, y: 4, z: 4, core: 2. Of those that a mesh axis runs over, the one named last changes fastest.
Arguments:
- coords: float32 [2048, 3, 512], P('leaf'), may hold values from 0 to 1
- charges: float32 [2048, 4, 512], P('leaf'), may hold values from -6 to 6
- bases: float32 [2048, 64, 512], P('leaf'), may hold values from -0.25 to 0.25
- up_transfer: float32 [2048, 64, 64], P('leaf'), may hold values from -0.25 to 0.25
- top_transfer: float32 [256, 64, 64], P('leaf'), may hold values from -0.75 to 0.75
- proxy_mid: float32 [256, 3, 64], replicated, may hold values from 0 to 1
- proxy_top: float32 [32, 3, 64], replicated, may hold values from 0 to 1
- near_list: int32 [2048, 4], P('leaf'), may hold values from 0 to 2047, as said below
- near_count: int32 [2048], P('leaf'), may hold values from 1 to 4
- far_mid: int32 [256, 32], replicated, may hold values from 0 to 255, as said below
- far_mid_count: int32 [256], replicated, may hold values from 16 to 32
- far_top: int32 [32, 6], replicated, may hold values from 0 to 31, as said below
- far_top_count: int32 [32], replicated, may hold values from 1 to 6
Outputs:
- field: float32 [2048, 4, 512], P('leaf')
The draws below stay inside these ranges and needn't reach their ends.
Inputs may be any that keep to these rules, and one draw needn't show every extreme that they name: `near_list`: slot 0 of leaf l's list is l itself; the slots of a list are distinct; with 16 leaves a device in Morton order, every entry of a leaf held by device d names a leaf of device d, one of the last 8 leaves of device d - 1 or one of the first 8 leaves of device d + 1. `far_mid`: the slots of a row are distinct nodes other than the row's own node. `far_top`: the slots of a row are distinct nodes other than the row's own node.
All inputs are finite; a program needn't handle non-finite values.
Results may differ from the reference program's by a relative error of at most 0.0003.
Values sent between devices are 32-bit elements; how exact they have to be, the bound alone decides.
No kernel may reach another device: no remote copies, remote signals or barrier semaphores. Data moves between devices by JAX's collectives and lax.ppermute only.
A program may use at most 64 MiB of HBM per device.

```python
import jax
import jax.numpy as jnp
from jax import lax

LEAF = 512
RANK = 64
NRHS = 4
NEAR = 4
EDGE = 8
FAR1 = 32
FAR2 = 6
LEAVES_DEV = 16
NLEAF = 2048
NP1 = 256
NP2 = 32


def draw_near_list(key, part):
    leaf_ids = jnp.arange(NLEAF)
    owner = leaf_ids // LEAVES_DEV
    span_width = LEAVES_DEV + 2 * EDGE
    slot_ids = jnp.arange(span_width)[None, :]
    candidates = owner[:, None] * LEAVES_DEV - EDGE + slot_ids
    usable = (candidates >= 0) & (candidates < NLEAF) & (candidates != leaf_ids[:, None])
    scores = jax.random.randint(key, (NLEAF, span_width), 0, 1 << 16) * span_width + slot_ids
    scores = jnp.where(usable, scores, (1 << 16) * span_width + slot_ids)
    order = jnp.argsort(scores, axis=1)[:, :NEAR - 1]
    others = jnp.take_along_axis(candidates, order, axis=1)
    return jnp.concatenate([leaf_ids[:, None], others], axis=1).astype(jnp.int32)


def pick_far(key, nodes, slots):
    keys = jax.random.split(key, nodes)
    shuffled = jax.vmap(lambda sub_key: jax.random.permutation(sub_key, nodes - 1))(keys)[:, :slots]
    target_ids = jnp.arange(nodes)[:, None]
    return jnp.where(shuffled >= target_ids, shuffled + 1, shuffled).astype(jnp.int32)


def draw_far_mid(key, part):
    return pick_far(jax.random.fold_in(key, 11), NP1, FAR1)


def draw_far_top(key, part):
    return pick_far(jax.random.fold_in(key, 23), NP2, FAR2)


def place_ends(result, key, least, largest):
    index_at = [jax.random.randint(jax.random.fold_in(key, axis), (), 0, length) for axis, length in enumerate(result.shape)]
    main_axis = result.shape.index(max(result.shape))
    beside = index_at[:main_axis] + [(index_at[main_axis] + 1) % result.shape[main_axis]] + index_at[main_axis + 1:]
    return result.at[tuple(index_at)].set(least).at[tuple(beside)].set(largest)


def block_levels(stream_key, extent, cuts, low, top_value):
    def one(dim, blocks):
        steps = jax.random.uniform(jax.random.fold_in(jax.random.fold_in(stream_key, 6), dim), (blocks,), jnp.float32, low / len(cuts), top_value / len(cuts))
        return jnp.repeat(jnp.exp(steps), extent[dim] // blocks).reshape((-1,) + (1,) * (len(extent) - dim - 1))

    factor_of = one(*cuts[0])
    for cut in cuts[1:]:
        factor_of = factor_of * one(*cut)
    return factor_of


def scatter_about(key, shape, deviation, limit, pieces=(), dtype=jnp.bfloat16):
    loudness = block_levels(key, shape, pieces, -0.22, 0.18) if pieces else 1.0
    values = jax.random.normal(key, shape, jnp.float32) * deviation * loudness
    return jnp.minimum(jnp.maximum(values, -limit), limit).astype(dtype)


def setup_inputs(seed: int = 0) -> dict:
    splits = jax.random.split(jax.random.key(seed), 14)
    coords = jnp.clip(1.0 * jax.random.uniform(splits[0], (NLEAF, 3, LEAF), jnp.float32) ** block_levels(splits[0], (NLEAF, 3, LEAF), ((0, 128),), -0.2, 0.2), 0.0, 1.0)
    charges = scatter_about(splits[1], (NLEAF, NRHS, LEAF), 1.0, 6.0, ((0, 128),), jnp.float32)
    bases = scatter_about(splits[2], (NLEAF, RANK, LEAF), LEAF ** -0.5, 0.25, ((0, 128),), jnp.float32)
    up_transfer = scatter_about(splits[3], (NLEAF, RANK, RANK), (8 * RANK) ** -0.5, 0.25, ((0, 128),), jnp.float32)
    top_transfer = scatter_about(splits[4], (NP1, RANK, RANK), RANK ** -0.5, 0.75, ((0, 128),), jnp.float32)
    proxy_mid = jnp.clip(jax.random.uniform(splits[5], (NP1, 3, RANK), jnp.float32, 0.0, 1.0), 0.0, 1.0)
    proxy_top = jnp.clip(jax.random.uniform(splits[6], (NP2, 3, RANK), jnp.float32, 0.0, 1.0), 0.0, 1.0)
    near_list = draw_near_list(jax.random.fold_in(splits[13], 71), 0)
    near_count = place_ends(jax.random.randint(splits[8], (NLEAF,), 1, NEAR + 1), jax.random.fold_in(splits[8], 1), 1, NEAR).astype(jnp.int32)
    far_mid = draw_far_mid(jax.random.fold_in(splits[13], 71), 0)
    far_mid_count = place_ends(jax.random.randint(splits[10], (NP1,), FAR1 // 2, FAR1 + 1), jax.random.fold_in(splits[10], 1), FAR1 // 2, FAR1).astype(jnp.int32)
    far_top = draw_far_top(jax.random.fold_in(splits[13], 71), 0)
    far_top_count = place_ends(jax.random.randint(splits[12], (NP2,), 1, FAR2 + 1), jax.random.fold_in(splits[12], 1), 1, FAR2).astype(jnp.int32)
    return {"coords": coords, "charges": charges, "bases": bases, "up_transfer": up_transfer, "top_transfer": top_transfer, "proxy_mid": proxy_mid, "proxy_top": proxy_top, "near_list": near_list, "near_count": near_count, "far_mid": far_mid, "far_mid_count": far_mid_count, "far_top": far_top, "far_top_count": far_top_count}


length_scale = 0.4
out_scale = 0.125
precise = lax.Precision.HIGHEST

def kernel(target_pts, source_pts):
    offset = target_pts[:, :, None] - source_pts[:, None, :]
    return jnp.exp(-jnp.sqrt(lax.optimization_barrier(jnp.sum(offset * offset, axis=0))) / length_scale)

def couple(target_proxy, source_proxy, coeffs, source_lists, counts):

    def single_target(packed_args):
        target_pts, source_ids, live_count = packed_args
        kernels = jax.vmap(kernel, (None, 0))(target_pts, source_proxy[source_ids])
        live_mask = (jnp.arange(source_ids.shape[0]) < live_count).astype(jnp.float32)
        return jnp.einsum('jab,jbk->ak', kernels * live_mask[:, None, None], coeffs[source_ids], precision=precise)
    return lax.map(single_target, (target_proxy, source_lists, counts))

def reference(coords, charges, bases, up_transfer, top_transfer, proxy_mid, proxy_top, near_list, near_count, far_mid, far_mid_count, far_top, far_top_count):
    leaf_coeffs = jnp.einsum('lrp,lkp->lrk', bases, charges, precision=precise)
    lifted_leaf = jnp.einsum('lrs,lsk->lrk', up_transfer, leaf_coeffs, precision=precise)
    mid_coeffs = lifted_leaf.reshape(NP1, 8, RANK, NRHS).sum(1)
    lifted_mid = jnp.einsum('nrs,nsk->nrk', top_transfer, mid_coeffs, precision=precise)
    top_coeffs = lifted_mid.reshape(NP2, 8, RANK, NRHS).sum(1)
    top_field = couple(proxy_top, proxy_top, top_coeffs, far_top, far_top_count)
    mid_far = couple(proxy_mid, proxy_mid, mid_coeffs, far_mid, far_mid_count)
    mid_field = mid_far + jnp.einsum('nsr,nsk->nrk', top_transfer, jnp.repeat(top_field, 8, axis=0), precision=precise)
    leaf_field = jnp.einsum('nsr,nsk->nrk', up_transfer, jnp.repeat(mid_field, 8, axis=0), precision=precise)
    far_part = jnp.einsum('lrp,lrk->lkp', bases, leaf_field, precision=precise)

    def near_leaf(packed_args):
        target_pts, source_ids, live_count = packed_args
        blocks = jax.vmap(kernel, (None, 0))(target_pts, coords[source_ids])
        live_mask = (jnp.arange(source_ids.shape[0]) < live_count).astype(jnp.float32)
        source_vals = charges[source_ids] * live_mask[:, None, None]
        return jnp.einsum('jts,jks->kt', blocks, source_vals, precision=precise)
    near_part = lax.map(near_leaf, (coords, near_list, near_count))
    return (near_part + far_part) * out_scale
```

```python
import functools

import jax
import jax.numpy as jnp
from jax import lax
from jax.experimental import pallas as pl
from jax.experimental.pallas import tpu as pltpu
from jax.sharding import PartitionSpec as P

EDGE = 8
NRHS = 4
length_scale = 0.4
out_scale = 0.125
TINY = 1e-30
RATE = -1.4426950408889634 / length_scale
NT = (((1,), (1,)), ((), ()))
TN = (((0,), (0,)), ((), ()))
bf16 = jnp.bfloat16
f32 = jnp.float32
VM = pl.BlockSpec(memory_space=pltpu.VMEM)
SM = pl.BlockSpec(memory_space=pltpu.SMEM)
ANY = pl.BlockSpec(memory_space=pl.ANY)
VMEM_LIMIT = 56 * 2**20


def snap(value, magic):
    return (value + magic) - magic


def split2(value):
    high = value.astype(bf16)
    return high, (value - high.astype(f32)).astype(bf16)


def rows8(value):
    high, low = split2(value)
    return jnp.concatenate([high.astype(f32), low.astype(f32)], axis=0).astype(bf16)


def fold8(value):
    return value[0:NRHS] + value[NRHS : 2 * NRHS]


def dot2(rows, value, dims):
    high, low = split2(value)
    return lax.dot_general(rows, high, dims, preferred_element_type=f32) + lax.dot_general(
        rows, low, dims, preferred_element_type=f32
    )


def features(points):
    x = points - 0.5
    h = snap(x, 49152.0)
    low = x - h
    l0 = snap(low, 96.0)
    l1 = low - l0
    n = jnp.sum(h * h, axis=0, keepdims=True)
    n0 = snap(n, 49152.0)
    n1 = n - n0
    m = jnp.sum(low * (h + h + low), axis=0, keepdims=True)
    m0 = snap(m, 384.0)
    rest = m - m0
    m1 = snap(rest, 1.5)
    m2 = rest - m1
    one = jnp.ones_like(n0)
    return jnp.concatenate([h, n0, n1, one, one, m0, l0, l1, m1, m2], axis=0).astype(bf16)


def mixing():
    r = lax.broadcasted_iota(jnp.int32, (16, 64), 0)
    c = lax.broadcasted_iota(jnp.int32, (16, 64), 1)
    h, l0, l1 = (0, 1, 2), (8, 9, 10), (11, 12, 13)
    n0, n1, one, other, m0, m1, m2 = 3, 4, 5, 6, 7, 14, 15
    entries = []
    for k in range(3):
        entries += [(0, h[k], h[k], -2.0)]
        entries += [(1, h[k], l0[k], -2.0), (1, l0[k], h[k], -2.0), (1, l1[k], h[k], -2.0)]
        entries += [(2, h[k], l1[k], -2.0), (2, l0[k], l0[k], -2.0), (2, l1[k], l0[k], -2.0)]
        entries += [(3, l0[k], l1[k], -2.0), (3, l1[k], l1[k], -2.0)]
    entries += [(0, n0, one, 1.0), (0, n1, one, 1.0), (0, one, n0, 1.0), (0, other, n1, 1.0)]
    entries += [(1, m0, one, 1.0), (1, m1, one, 1.0), (1, m2, one, 1.0)]
    entries += [(1, one, m0, 1.0), (1, other, m1, 1.0), (2, one, m2, 1.0)]
    out = jnp.zeros((16, 64), f32)
    for block, source, target, value in entries:
        out = jnp.where((r == target) & (c == 16 * block + source), value, out)
    return out.astype(bf16)


def targets_of(feature_rows, mix):
    return lax.dot_general(feature_rows, mix, TN, preferred_element_type=f32).astype(bf16)


def covariance(squared):
    y = jnp.maximum(squared, TINY)
    return jnp.exp2(y * lax.rsqrt(y) * RATE)


def up_body(coords, charges, bases, up_transfer, top_transfer, tile, first, last):
    leaves = coords.shape[0]
    edge = first.shape[0]
    for ref, start in ((first, 0), (last, leaves - edge)):
        ref[:, 0:3, :] = coords[start : start + edge]
        ref[:, 3:4, :] = jnp.zeros((edge, 1, coords.shape[2]), f32)
        ref[:, 4:8, :] = charges[start : start + edge]
    mids = []
    lift = None
    for n in range(leaves // 8):
        mid = None
        for leaf in range(8 * n, 8 * n + 8):
            coeffs = fold8(dot2(rows8(charges[leaf]), bases[leaf], NT))
            part = fold8(dot2(rows8(coeffs), up_transfer[leaf], NT))
            mid = part if mid is None else mid + part
        mids.append(mid)
        part = fold8(dot2(rows8(mid), top_transfer[n], NT))
        lift = part if lift is None else lift + part
    tile[0:4, :] = jnp.concatenate(mids, axis=1)
    tile[4:8, :] = jnp.concatenate([lift, jnp.zeros_like(lift)], axis=1)


def up_call(coords, charges, bases, up_transfer, top_transfer):
    points = coords.shape[2]
    halo = jax.ShapeDtypeStruct((EDGE, 8, points), f32)
    return pl.pallas_call(
        up_body,
        out_shape=(jax.ShapeDtypeStruct((8, 128), f32), halo, halo),
        in_specs=[VM] * 5,
        out_specs=(VM, VM, VM),
        compiler_params=pltpu.CompilerParams(vmem_limit_bytes=VMEM_LIMIT),
        name="upward",
    )(coords, charges, bases, up_transfer, top_transfer)


def near_body(
    near_list,
    near_count,
    coords,
    charges,
    before,
    after,
    out,
    target_rows,
    source_rows,
    source_vals,
    square_a,
    square_b,
    kern_a,
    kern_b,
    total_rows,
    pair_t,
    pair_s,
    *,
    chunk,
    unroll,
):
    leaves, _, points = coords.shape
    edge = before.shape[0]
    slots = near_list.shape[1]
    window_start = lax.axis_index("leaf") * leaves - edge
    total = 0
    for t in range(leaves):
        for j in range(slots):
            pair_t[total + j] = t
            pair_s[total + j] = near_list[t, j] - window_start
        total = total + near_count[t]
    for j in range(unroll + 1):
        pair_t[total + j] = leaves
        pair_s[total + j] = 0
    mix = mixing()

    def put(slot, pts, vals):
        rows = features(pts)
        for b in range(4):
            source_rows[slot, 16 * b : 16 * b + 16, :] = rows
        source_vals[slot] = rows8(vals)
        return rows

    def own(i, _):
        target_rows[i] = targets_of(put(edge + i, coords[i], charges[i]), mix)
        return 0

    lax.fori_loop(0, leaves, own, 0, unroll=2)

    def halo(i, _):
        put(i, before[i, 0:3, :], before[i, 4:8, :])
        put(edge + leaves + i, after[i, 0:3, :], after[i, 4:8, :])
        return 0

    lax.fori_loop(0, edge, halo, 0)
    target_rows[leaves] = jnp.zeros((points, 64), bf16)
    total_rows[...] = jnp.zeros_like(total_rows)
    kern_b[...] = jnp.zeros_like(kern_b)

    def distances(i, dst, c):
        dst[c : c + chunk, :] = jnp.dot(
            target_rows[pair_t[i], c : c + chunk, :], source_rows[pair_s[i]], preferred_element_type=f32
        )

    def kernels(src, dst, c):
        high, low = split2(covariance(src[c : c + chunk, :]))
        dst[0, c : c + chunk, :] = high
        dst[1, c : c + chunk, :] = low

    def apply(i, src, c):
        vals = source_vals[pair_s[i]]
        total_rows[pair_t[i], :, c : c + chunk] += lax.dot_general(
            vals, src[0, c : c + chunk, :], NT, preferred_element_type=f32
        ) + lax.dot_general(vals, src[1, c : c + chunk, :], NT, preferred_element_type=f32)

    chunks = range(0, points, chunk)
    for c in chunks:
        distances(0, square_a, c)

    def step(k, _):
        i = unroll * k
        previous = jnp.where(k == 0, total, i - 1)
        for u in range(0, unroll, 2):
            for c in chunks:
                kernels(square_a, kern_a, c)
                distances(i + u + 1, square_b, c)
                apply(previous if u == 0 else i + u - 1, kern_b, c)
            for c in chunks:
                kernels(square_b, kern_b, c)
                distances(i + u + 2, square_a, c)
                apply(i + u, kern_a, c)
        return 0

    trips = (total + unroll - 1) // unroll
    lax.fori_loop(0, trips, step, 0)
    for c in chunks:
        apply(unroll * trips - 1, kern_b, c)

    def finish(i, _):
        out[i] = fold8(total_rows[i])
        return 0

    lax.fori_loop(0, leaves, finish, 0, unroll=4)


def near_call(near_list, near_count, coords, charges, before, after, chunk=128, unroll=4):
    leaves, _, points = coords.shape
    window = leaves + 2 * EDGE
    pairs = near_list.shape[1] * leaves + unroll + 4
    return pl.pallas_call(
        functools.partial(near_body, chunk=chunk, unroll=unroll),
        out_shape=jax.ShapeDtypeStruct((leaves, NRHS, points), f32),
        in_specs=[SM, SM, VM, VM, VM, VM],
        out_specs=VM,
        scratch_shapes=[
            pltpu.VMEM((leaves + 1, points, 64), bf16),
            pltpu.VMEM((window, 64, points), bf16),
            pltpu.VMEM((window, 2 * NRHS, points), bf16),
            pltpu.VMEM((points, points), f32),
            pltpu.VMEM((points, points), f32),
            pltpu.VMEM((2, points, points), bf16),
            pltpu.VMEM((2, points, points), bf16),
            pltpu.VMEM((leaves + 1, 2 * NRHS, points), f32),
            pltpu.SMEM((pairs,), jnp.int32),
            pltpu.SMEM((pairs,), jnp.int32),
        ],
        compiler_params=pltpu.CompilerParams(vmem_limit_bytes=VMEM_LIMIT),
        name="near",
    )(near_list, near_count, coords, charges, before, after)


def far_body(
    far_mid,
    mid_count,
    far_top,
    top_count,
    gathered,
    near,
    bases,
    up_transfer,
    top_transfer,
    proxy_mid,
    proxy_top,
    out,
    mid_ids,
    top_ids,
    pts,
    coef,
    sems,
):
    leaves = near.shape[0]
    nodes = leaves // 8
    rank = bases.shape[1]
    device = lax.axis_index("leaf")
    own = device * nodes
    parent = own // 8
    mid_row = (own // 8) * 8
    top_row = (parent // 8) * 8
    copies = (
        pltpu.make_async_copy(far_mid.at[pl.ds(pl.multiple_of(mid_row, 8), 8), :], mid_ids, sems.at[0]),
        pltpu.make_async_copy(far_top.at[pl.ds(pl.multiple_of(top_row, 8), 8), :], top_ids, sems.at[1]),
    )
    for copy in copies:
        copy.start()
    for copy in copies:
        copy.wait()
    mix = mixing()
    lane = lax.broadcasted_iota(jnp.int32, (NRHS, 2 * rank), 1)

    def field(target, ids, row, count, proxy, coeffs_of):
        slots = ids.shape[1]
        for j in range(0, slots, 2):
            a, b = ids[row, j], ids[row, j + 1]
            at = slice(rank * j, rank * j + 2 * rank)
            pts[0:3, at] = jnp.concatenate([proxy[a], proxy[b]], axis=1)
            left = jnp.where(j < count, coeffs_of(a, 0), 0.0)
            right = jnp.where(j + 1 < count, coeffs_of(b, 1), 0.0)
            coef[:, at] = jnp.where(lane < rank, left, right)
        width = rank * slots
        rows = features(pts[0:3, 0:width])
        squared = jnp.dot(
            targets_of(features(target), mix), jnp.concatenate([rows] * 4, axis=0), preferred_element_type=f32
        )
        return fold8(dot2(rows8(coef[:, 0:width]), covariance(squared), NT))

    def mid_coeffs(s, half):
        node = gathered[s // 2, 0:NRHS, :]
        return jnp.where(s % 2 == half, node, pltpu.roll(node, rank, 1))

    def top_coeffs(s, half):
        node = gathered[4 * s, NRHS : 2 * NRHS, :]
        for k in range(1, 4):
            node = node + gathered[4 * s + k, NRHS : 2 * NRHS, :]
        return node if half == 0 else pltpu.roll(node, rank, 1)

    top_field = field(proxy_top[parent], top_ids, parent - top_row, top_count[parent], proxy_top, top_coeffs)
    top8 = rows8(top_field)
    for n in range(nodes):
        mid_field = field(
            proxy_mid[own + n], mid_ids, own - mid_row + n, mid_count[own + n], proxy_mid, mid_coeffs
        )
        mid_field = mid_field + fold8(dot2(top8, top_transfer[n], (((1,), (0,)), ((), ()))))
        mid8 = rows8(mid_field)
        for leaf in range(8 * n, 8 * n + 8):
            leaf_field = fold8(dot2(mid8, up_transfer[leaf], (((1,), (0,)), ((), ()))))
            far = fold8(dot2(rows8(leaf_field), bases[leaf], (((1,), (0,)), ((), ()))))
            out[leaf] = (near[leaf] + far) * out_scale


def far_call(
    far_mid, mid_count, far_top, top_count, gathered, near, bases, up_transfer, top_transfer, proxy_mid, proxy_top
):
    width = bases.shape[1] * max(far_mid.shape[1], far_top.shape[1])
    return pl.pallas_call(
        far_body,
        out_shape=jax.ShapeDtypeStruct(near.shape, f32),
        in_specs=[ANY, SM, ANY, SM] + [VM] * 7,
        out_specs=VM,
        scratch_shapes=[
            pltpu.SMEM((8, far_mid.shape[1]), jnp.int32),
            pltpu.SMEM((8, far_top.shape[1]), jnp.int32),
            pltpu.VMEM((8, width), f32),
            pltpu.VMEM((NRHS, width), f32),
            pltpu.SemaphoreType.DMA((2,)),
        ],
        compiler_params=pltpu.CompilerParams(vmem_limit_bytes=VMEM_LIMIT),
        name="far",
    )(far_mid, mid_count, far_top, top_count, gathered, near, bases, up_transfer, top_transfer, proxy_mid, proxy_top)


def shards(
    coords,
    charges,
    bases,
    up_transfer,
    top_transfer,
    proxy_mid,
    proxy_top,
    near_list,
    near_count,
    far_mid,
    far_mid_count,
    far_top,
    far_top_count,
):
    peers = lax.axis_size("leaf")
    up = [(i, i + 1) for i in range(peers - 1)]
    down = [(j, i) for i, j in up]
    tile, first, last = up_call(coords, charges, bases, up_transfer, top_transfer)
    before = lax.ppermute(last, "leaf", up)
    after = lax.ppermute(first, "leaf", down)
    copies = jnp.broadcast_to(tile, (peers,) + tile.shape)
    gathered = lax.all_to_all(copies, "leaf", 0, 0, tiled=True)
    near = near_call(near_list, near_count, coords, charges, before, after)
    return far_call(
        far_mid,
        far_mid_count,
        far_top,
        far_top_count,
        gathered,
        near,
        bases,
        up_transfer,
        top_transfer,
        proxy_mid,
        proxy_top,
    )


def solution(mesh):
    placed = (
        P("leaf", None, None),
        P("leaf", None, None),
        P("leaf", None, None),
        P("leaf", None, None),
        P("leaf", None, None),
        P(),
        P(),
        P("leaf", None),
        P("leaf"),
        P(),
        P(),
        P(),
        P(),
    )
    return jax.shard_map(
        shards, mesh=mesh, in_specs=placed, out_specs=P("leaf", None, None), check_vma=False
    )
```

```python
import functools

import jax
import jax.numpy as jnp
from jax import lax
from jax.experimental import pallas as pl
from jax.experimental.pallas import tpu as pltpu
from jax.sharding import PartitionSpec as P


EDGE = 8
NRHS = 4
length_scale = 0.4
out_scale = 0.125
TINY = 1e-30
RATE = -1.4426950408889634 / length_scale
NT = (((1,), (1,)), ((), ()))
TN = (((0,), (0,)), ((), ()))
bf16 = jnp.bfloat16
f32 = jnp.float32
VM = pl.BlockSpec(memory_space=pltpu.VMEM)
HBM = pl.BlockSpec(memory_space=pltpu.HBM)
VMEM_LIMIT = 56 * 2**20


def snap(value, magic):
    return (value + magic) - magic


def split2(value):
    high = value.astype(bf16)
    return high, (value - high.astype(f32)).astype(bf16)


def rows8(value):
    high, low = split2(value)
    return jnp.concatenate([high.astype(f32), low.astype(f32)], axis=0).astype(bf16)


def fold8(value):
    return value[0:NRHS] + value[NRHS : 2 * NRHS]


def dot2(rows, value, dims):
    high, low = split2(value)
    return lax.dot_general(rows, high, dims, preferred_element_type=f32) + lax.dot_general(
        rows, low, dims, preferred_element_type=f32
    )


def pieces(x0, x1, x2, put):
    n = m = None
    for k, points in enumerate((x0, x1, x2)):
        x = points - 0.5
        h = snap(x, 49152.0)
        low = x - h
        l0 = snap(low, 96.0)
        put(k, h)
        put(8 + k, l0)
        put(11 + k, low - l0)
        n = h * h if n is None else n + h * h
        part = low * (h + h + low)
        m = part if m is None else m + part
    n0 = snap(n, 49152.0)
    m0 = snap(m, 384.0)
    m1 = snap(m - m0, 1.5)
    for row, value in ((3, n0), (4, n - n0), (7, m0), (14, m1), (15, m - m0 - m1)):
        put(row, value)
    one = jnp.ones_like(n)
    put(5, one)
    put(6, one)


def features(points):
    rows = [None] * 16

    def put(row, value):
        rows[row] = value

    pieces(points[0:1], points[1:2], points[2:3], put)
    return jnp.concatenate(rows, axis=0).astype(bf16)


def mixing():
    r = lax.broadcasted_iota(jnp.int32, (16, 64), 0)
    c = lax.broadcasted_iota(jnp.int32, (16, 64), 1)
    h, l0, l1 = (0, 1, 2), (8, 9, 10), (11, 12, 13)
    n0, n1, one, other, m0, m1, m2 = 3, 4, 5, 6, 7, 14, 15
    entries = []
    for k in range(3):
        entries += [(0, h[k], h[k], -2.0)]
        entries += [(1, h[k], l0[k], -2.0), (1, l0[k], h[k], -2.0), (1, l1[k], h[k], -2.0)]
        entries += [(2, h[k], l1[k], -2.0), (2, l0[k], l0[k], -2.0), (2, l1[k], l0[k], -2.0)]
        entries += [(3, l0[k], l1[k], -2.0), (3, l1[k], l1[k], -2.0)]
    entries += [(0, n0, one, 1.0), (0, n1, one, 1.0), (0, one, n0, 1.0), (0, other, n1, 1.0)]
    entries += [(1, m0, one, 1.0), (1, m1, one, 1.0), (1, m2, one, 1.0)]
    entries += [(1, one, m0, 1.0), (1, other, m1, 1.0), (2, one, m2, 1.0)]
    out = jnp.zeros((16, 64), f32)
    for block, source, target, value in entries:
        out = jnp.where((r == target) & (c == 16 * block + source), value, out)
    return out.astype(bf16)


def targets_of(feature_rows, mix):
    return lax.dot_general(feature_rows, mix, TN, preferred_element_type=f32).astype(bf16)


def covariance(squared):
    y = jnp.maximum(squared, TINY)
    return jnp.exp2(y * lax.rsqrt(y) * RATE)


def up_body(
    coords_hbm,
    charges_hbm,
    bases_hbm,
    up_hbm,
    top_hbm,
    copies_hbm,
    beside_hbm,
    across_hbm,
    coords,
    charges,
    bases,
    up_transfer,
    top_transfer,
    copies,
    beside,
    across,
    sems,
    group_sems,
):
    leaves = charges.shape[0]
    edge = beside.shape[1]
    group = 4
    small = [
        pltpu.make_async_copy(src, dst, sems.at[k])
        for k, (src, dst) in enumerate(((charges_hbm, charges), (coords_hbm, coords), (top_hbm, top_transfer)))
    ]
    moves = []
    for g in range(leaves // group):
        at = pl.ds(group * g, group)
        moves.append(
            (
                pltpu.make_async_copy(bases_hbm.at[at], bases.at[at], group_sems.at[0, g]),
                pltpu.make_async_copy(up_hbm.at[at], up_transfer.at[at], group_sems.at[1, g]),
            )
        )
    for move in small[0:2] + [m for pair in moves for m in pair] + small[2:]:
        move.start()
    small[0].wait()
    small[1].wait()
    odd = lax.axis_index("leaf") % 2
    sends = []
    for k, (ref, start) in enumerate(((beside, (1 - odd) * (leaves - edge)), (across, odd * (leaves - edge)))):
        start = pl.multiple_of(start, edge)
        for c in range(3):
            ref[c] = coords[c, pl.ds(start, edge), :]
        ref[3] = jnp.zeros(ref.shape[1:], f32)
        for g in range(4):
            ref[4 + g, 0:4, :] = charges[start + 2 * g]
            ref[4 + g, 4:8, :] = charges[start + 2 * g + 1]
        sends.append(pltpu.make_async_copy(ref, (beside_hbm, across_hbm)[k], sems.at[3 + k]))
        sends[k].start()
    mids = []
    lift = None
    for n in range(leaves // 8):
        mid = None
        for g in range(2 * n, 2 * n + 2):
            for move in moves[g]:
                move.wait()
            for leaf in range(group * g, group * g + group):
                coeffs = fold8(dot2(rows8(charges[leaf]), bases[leaf], NT))
                part = fold8(dot2(rows8(coeffs), up_transfer[leaf], NT))
                mid = part if mid is None else mid + part
        mids.append(mid)
        if n == 0:
            small[2].wait()
        part = fold8(dot2(rows8(mid), top_transfer[n], NT))
        lift = part if lift is None else lift + part
    tile = jnp.concatenate(
        [jnp.concatenate(mids, axis=1), jnp.concatenate([lift, jnp.zeros_like(lift)], axis=1)], axis=0
    )
    copies[...] = jnp.broadcast_to(tile, copies.shape)
    sends.append(pltpu.make_async_copy(copies, copies_hbm, sems.at[5]))
    sends[2].start()
    for send in sends:
        send.wait()


def up_call(peers, coords, charges, bases, up_transfer, top_transfer):
    halo = (8, EDGE, coords.shape[2])
    copies = (peers, 8, 128)
    args = (coords, charges, bases, up_transfer, top_transfer)
    return pl.pallas_call(
        up_body,
        out_shape=tuple(jax.ShapeDtypeStruct(shape, f32) for shape in (copies, halo, halo)),
        in_specs=[HBM] * 5,
        out_specs=(HBM, HBM, HBM),
        scratch_shapes=[pltpu.VMEM(a.shape, f32) for a in args]
        + [pltpu.VMEM(shape, f32) for shape in (copies, halo, halo)]
        + [pltpu.SemaphoreType.DMA((6,)), pltpu.SemaphoreType.DMA((2, 4))],
        compiler_params=pltpu.CompilerParams(vmem_limit_bytes=VMEM_LIMIT),
        name="upward",
    )(*args)


def near_body(
    list_hbm,
    count_hbm,
    coords_hbm,
    charges_hbm,
    beside,
    across,
    out,
    near_list,
    near_count,
    coords,
    charges,
    target_rows,
    source_rows,
    source_vals,
    feature_rows,
    square_a,
    square_b,
    kern_a,
    kern_b,
    total_rows,
    pair_t,
    pair_s,
    sems,
    *,
    chunk,
    unroll,
):
    leaves, _, points = charges.shape
    edge = beside.shape[1]
    slots = near_list.shape[0]
    pairs_of = ((coords_hbm, coords), (list_hbm, near_list), (count_hbm, near_count), (charges_hbm, charges))
    moves = [pltpu.make_async_copy(src, dst, sems.at[k]) for k, (src, dst) in enumerate(pairs_of)]
    for move in moves:
        move.start()
    window_start = lax.axis_index("leaf") * leaves - edge
    odd = lax.axis_index("leaf") % 2
    beside_at = (1 - odd) * (edge + leaves)
    across_at = odd * (edge + leaves)
    mix = mixing()
    target_rows[leaves] = jnp.zeros((points, 64), bf16)
    total_rows[...] = jnp.zeros_like(total_rows)
    kern_b[...] = jnp.zeros_like(kern_b)
    for move in moves:
        move.wait()
    total = 0
    for t in range(leaves):
        for j in range(slots):
            pair_t[total + j] = t
            pair_s[total + j] = near_list[j, t] - window_start
        total = total + near_count[t]
    for j in range(unroll + 1):
        pair_t[total + j] = leaves
        pair_s[total + j] = 0
    for ref, base, count in ((beside, beside_at, edge), (across, across_at, edge), (coords, edge, leaves)):

        def put(row, value):
            for q in range(points // 128):
                feature_rows.at[q][pl.ds(16 * base + row, count, stride=16), :] = value[:, 128 * q : 128 * q + 128]

        pieces(ref[0], ref[1], ref[2], put)

    def rows_of(slot):
        at = pl.ds(pl.multiple_of(16 * slot, 16), 16)
        rows = jnp.concatenate([feature_rows[q, at, :].astype(bf16) for q in range(points // 128)], axis=1)
        for b in range(4):
            source_rows[slot, 16 * b : 16 * b + 16, :] = rows
        return rows

    def own(i, _):
        target_rows[i] = targets_of(rows_of(edge + i), mix)
        source_vals[edge + i] = rows8(charges[i])
        return 0

    lax.fori_loop(0, leaves, own, 0, unroll=4)

    def halo(g, _):
        for ref, base in ((beside, beside_at), (across, across_at)):
            for k in range(2):
                rows_of(base + 2 * g + k)
                source_vals[base + 2 * g + k] = rows8(ref[4 + g, 4 * k : 4 * k + 4, :])
        return 0

    lax.fori_loop(0, edge // 2, halo, 0)

    def distances(i, dst, c):
        dst[c : c + chunk, :] = jnp.dot(
            target_rows[pair_t[i], c : c + chunk, :], source_rows[pair_s[i]], preferred_element_type=f32
        )

    def kernels(src, dst, c):
        high, low = split2(covariance(src[c : c + chunk, :]))
        dst[0, c : c + chunk, :] = high
        dst[1, c : c + chunk, :] = low

    def apply(i, src, c):
        vals = source_vals[pair_s[i]]
        total_rows[pair_t[i], :, c : c + chunk] += lax.dot_general(
            vals, src[0, c : c + chunk, :], NT, preferred_element_type=f32
        ) + lax.dot_general(vals, src[1, c : c + chunk, :], NT, preferred_element_type=f32)

    chunks = range(0, points, chunk)
    for c in chunks:
        distances(0, square_a, c)

    def step(k, _):
        i = unroll * k
        previous = jnp.where(k == 0, total, i - 1)
        for u in range(0, unroll, 2):
            for c in chunks:
                kernels(square_a, kern_a, c)
                distances(i + u + 1, square_b, c)
                apply(previous if u == 0 else i + u - 1, kern_b, c)
            for c in chunks:
                kernels(square_b, kern_b, c)
                distances(i + u + 2, square_a, c)
                apply(i + u, kern_a, c)
        return 0

    trips = (total + unroll - 1) // unroll
    lax.fori_loop(0, trips, step, 0)
    for c in chunks:
        apply(unroll * trips - 1, kern_b, c)

    def finish(i, _):
        out[i] = fold8(total_rows[i])
        return 0

    lax.fori_loop(0, leaves, finish, 0, unroll=4)


def near_call(near_list, near_count, coords, charges, beside, across, chunk=128, unroll=4):
    leaves, _, points = charges.shape
    window = leaves + 2 * EDGE
    pairs = near_list.shape[0] * leaves + unroll + 4
    return pl.pallas_call(
        functools.partial(near_body, chunk=chunk, unroll=unroll),
        out_shape=jax.ShapeDtypeStruct((leaves, NRHS, points), f32),
        in_specs=[HBM] * 4 + [VM] * 2,
        out_specs=VM,
        scratch_shapes=[
            pltpu.SMEM(near_list.shape, jnp.int32),
            pltpu.SMEM(near_count.shape, jnp.int32),
            pltpu.VMEM(coords.shape, f32),
            pltpu.VMEM(charges.shape, f32),
            pltpu.VMEM((leaves + 1, points, 64), bf16),
            pltpu.VMEM((window, 64, points), bf16),
            pltpu.VMEM((window, 2 * NRHS, points), bf16),
            pltpu.VMEM((points // 128, window * 16, 128), f32),
            pltpu.VMEM((points, points), f32),
            pltpu.VMEM((points, points), f32),
            pltpu.VMEM((2, points, points), bf16),
            pltpu.VMEM((2, points, points), bf16),
            pltpu.VMEM((leaves + 1, 2 * NRHS, points), f32),
            pltpu.SMEM((pairs,), jnp.int32),
            pltpu.SMEM((pairs,), jnp.int32),
            pltpu.SemaphoreType.DMA((4,)),
        ],
        compiler_params=pltpu.CompilerParams(vmem_limit_bytes=VMEM_LIMIT),
        name="near",
    )(near_list, near_count, coords, charges, beside, across)


def far_body(
    far_mid_hbm,
    mid_count_hbm,
    far_top_hbm,
    top_count_hbm,
    proxy_mid_hbm,
    proxy_top_hbm,
    top_hbm,
    up_hbm,
    bases_hbm,
    gathered,
    near,
    out,
    far_mid,
    mid_count,
    far_top,
    top_count,
    proxy_mid,
    proxy_top,
    top_transfer,
    up_transfer,
    bases,
    mid_points,
    top_points,
    pts,
    coef,
    sems,
):
    sources = (
        far_mid_hbm,
        mid_count_hbm,
        far_top_hbm,
        top_count_hbm,
        proxy_mid_hbm,
        proxy_top_hbm,
        top_hbm,
        up_hbm,
        bases_hbm,
    )
    places = (far_mid, mid_count, far_top, top_count, proxy_mid, proxy_top, top_transfer, up_transfer, bases)
    moves = [pltpu.make_async_copy(src, dst, sems.at[k]) for k, (src, dst) in enumerate(zip(sources, places))]
    for move in moves:
        move.start()
    leaves = near.shape[0]
    nodes = leaves // 8
    rank = bases.shape[1]
    device = lax.axis_index("leaf")
    own = device * nodes
    parent = own // 8
    for move in moves[0:6]:
        move.wait()
    for k in range(3):
        mids, tops = proxy_mid[k].T, proxy_top[k]
        mid_points[pl.ds(k, mids.shape[0], stride=4), :] = jnp.concatenate([mids, mids], axis=1)
        top_points[pl.ds(k, tops.shape[0], stride=4), :] = jnp.concatenate([tops, tops], axis=1)

    def proxy(ref, node):
        return ref[pl.ds(4 * node, 3), :]

    mix = mixing()
    lane = lax.broadcasted_iota(jnp.int32, (NRHS, 2 * rank), 1)

    def field(node, ids, count, nodes_points, coeffs_of):
        slots = ids.shape[0]
        for j in range(0, slots, 2):
            a, b = ids[j, node], ids[j + 1, node]
            at = slice(rank * j, rank * j + 2 * rank)
            pts[0:3, at] = jnp.where(lane[0:3] < rank, proxy(nodes_points, a), proxy(nodes_points, b))
            left = jnp.where(j < count, coeffs_of(a, 0), 0.0)
            right = jnp.where(j + 1 < count, coeffs_of(b, 1), 0.0)
            coef[:, at] = jnp.where(lane < rank, left, right)
        width = rank * slots
        rows = features(pts[0:3, 0:width])
        squared = jnp.dot(
            targets_of(features(proxy(nodes_points, node)[:, 0:rank]), mix), jnp.concatenate([rows] * 4, axis=0), preferred_element_type=f32
        )
        return fold8(dot2(rows8(coef[:, 0:width]), covariance(squared), NT))

    def mid_coeffs(s, half):
        node = gathered[s // 2, 0:NRHS, :]
        return jnp.where(s % 2 == half, node, pltpu.roll(node, rank, 1))

    def top_coeffs(s, half):
        node = gathered[4 * s, NRHS : 2 * NRHS, :]
        for k in range(1, 4):
            node = node + gathered[4 * s + k, NRHS : 2 * NRHS, :]
        return node if half == 0 else pltpu.roll(node, rank, 1)

    top_field = field(parent, far_top, top_count[parent], top_points, top_coeffs)
    top8 = rows8(top_field)
    for move in moves[6:]:
        move.wait()
    for n in range(nodes):
        mid_field = field(own + n, far_mid, mid_count[own + n], mid_points, mid_coeffs)
        mid_field = mid_field + fold8(dot2(top8, top_transfer[n], (((1,), (0,)), ((), ()))))
        mid8 = rows8(mid_field)
        for leaf in range(8 * n, 8 * n + 8):
            leaf_field = fold8(dot2(mid8, up_transfer[leaf], (((1,), (0,)), ((), ()))))
            far = fold8(dot2(rows8(leaf_field), bases[leaf], (((1,), (0,)), ((), ()))))
            out[leaf] = (near[leaf] + far) * out_scale


def far_call(
    far_mid, mid_count, far_top, top_count, proxy_mid, proxy_top, top_transfer, up_transfer, bases, gathered, near
):
    width = bases.shape[1] * max(far_mid.shape[0], far_top.shape[0])
    integers = (far_mid, mid_count, far_top, top_count)
    floats = (proxy_mid, proxy_top, top_transfer, up_transfer, bases)
    return pl.pallas_call(
        far_body,
        out_shape=jax.ShapeDtypeStruct(near.shape, f32),
        in_specs=[HBM] * 9 + [VM] * 2,
        out_specs=VM,
        scratch_shapes=[pltpu.SMEM(a.shape, jnp.int32) for a in integers]
        + [pltpu.VMEM(a.shape, f32) for a in floats]
        + [
            pltpu.VMEM((4 * proxy_mid.shape[2], 2 * proxy_mid.shape[1]), f32),
            pltpu.VMEM((4 * proxy_top.shape[1], 2 * proxy_top.shape[2]), f32),
            pltpu.VMEM((8, width), f32),
            pltpu.VMEM((NRHS, width), f32),
            pltpu.SemaphoreType.DMA((9,)),
        ],
        compiler_params=pltpu.CompilerParams(vmem_limit_bytes=VMEM_LIMIT),
        name="far",
    )(*integers, *floats, gathered, near)


def shards(
    coords,
    charges,
    bases,
    up_transfer,
    top_transfer,
    proxy_mid,
    proxy_top,
    near_list,
    near_count,
    far_mid,
    far_mid_count,
    far_top,
    far_top_count,
):
    peers = lax.axis_size("leaf")
    chip = [(i, i ^ 1) for i in range(peers)]
    next_chip = [(i, i + 1 if i % 2 else i - 1) for i in range(1, peers - 1)]
    coords = jnp.transpose(coords, (1, 0, 2))
    copies, beside, across = up_call(peers, coords, charges, bases, up_transfer, top_transfer)
    across = lax.ppermute(across, "leaf", next_chip)
    beside = lax.ppermute(beside, "leaf", chip)
    gathered = lax.all_to_all(copies, "leaf", 0, 0, tiled=True)
    near = near_call(near_list.T, near_count, coords, charges, beside, across)
    return far_call(
        far_mid.T,
        far_mid_count,
        far_top.T,
        far_top_count,
        jnp.transpose(proxy_mid, (1, 2, 0)),
        jnp.transpose(proxy_top, (1, 0, 2)),
        top_transfer,
        up_transfer,
        bases,
        gathered,
        near,
    )


def solution(mesh):
    placed = (
        P("leaf", None, None),
        P("leaf", None, None),
        P("leaf", None, None),
        P("leaf", None, None),
        P("leaf", None, None),
        P(),
        P(),
        P("leaf", None),
        P("leaf"),
        P(),
        P(),
        P(),
        P(),
    )
    return jax.shard_map(
        shards, mesh=mesh, in_specs=placed, out_specs=P("leaf", None, None), check_vma=False
    )
```

```python
import functools

import jax
import jax.numpy as jnp
from jax import lax
from jax.experimental import pallas as pl
from jax.experimental.pallas import tpu as pltpu
from jax.sharding import PartitionSpec as P


EDGE = 8
NRHS = 4
length_scale = 0.4
out_scale = 0.125
TINY = 1e-30
RATE = -1.4426950408889634 / length_scale
NT = (((1,), (1,)), ((), ()))
TN = (((0,), (0,)), ((), ()))
bf16 = jnp.bfloat16
f32 = jnp.float32
VM = pl.BlockSpec(memory_space=pltpu.VMEM)
HBM = pl.BlockSpec(memory_space=pltpu.HBM)
VMEM_LIMIT = 67043328
BLOCK = 128


def snap(value, magic):
    return (value + magic) - magic


def split2(value):
    high = value.astype(bf16)
    return high, (value - high.astype(f32)).astype(bf16)


def rows8(value):
    high, low = split2(value)
    return jnp.concatenate([high.astype(f32), low.astype(f32)], axis=0).astype(bf16)


def fold8(value):
    return value[0:NRHS] + value[NRHS : 2 * NRHS]


def dot2(rows, value, dims):
    high, low = split2(value)
    return lax.dot_general(rows, high, dims, preferred_element_type=f32) + lax.dot_general(
        rows, low, dims, preferred_element_type=f32
    )


def pieces(x0, x1, x2, put):
    n = m = None
    for k, points in enumerate((x0, x1, x2)):
        x = points - 0.5
        h = snap(x, 49152.0)
        low = x - h
        l0 = snap(low, 96.0)
        put(k, h)
        put(8 + k, l0)
        put(11 + k, low - l0)
        n = h * h if n is None else n + h * h
        part = low * (h + h + low)
        m = part if m is None else m + part
    n0 = snap(n, 49152.0)
    m0 = snap(m, 384.0)
    m1 = snap(m - m0, 1.5)
    for row, value in ((3, n0), (4, n - n0), (7, m0), (14, m1), (15, m - m0 - m1)):
        put(row, value)
    one = jnp.ones_like(n)
    put(5, one)
    put(6, one)


def features(points):
    rows = [None] * 16

    def put(row, value):
        rows[row] = value

    pieces(points[0:1], points[1:2], points[2:3], put)
    return jnp.concatenate(rows, axis=0).astype(bf16)


def mixing():
    r = lax.broadcasted_iota(jnp.int32, (16, 64), 0)
    c = lax.broadcasted_iota(jnp.int32, (16, 64), 1)
    h, l0, l1 = (0, 1, 2), (8, 9, 10), (11, 12, 13)
    n0, n1, one, other, m0, m1, m2 = 3, 4, 5, 6, 7, 14, 15
    entries = []
    for k in range(3):
        entries += [(0, h[k], h[k], -2.0)]
        entries += [(1, h[k], l0[k], -2.0), (1, l0[k], h[k], -2.0), (1, l1[k], h[k], -2.0)]
        entries += [(2, h[k], l1[k], -2.0), (2, l0[k], l0[k], -2.0), (2, l1[k], l0[k], -2.0)]
        entries += [(3, l0[k], l1[k], -2.0), (3, l1[k], l1[k], -2.0)]
    entries += [(0, n0, one, 1.0), (0, n1, one, 1.0), (0, one, n0, 1.0), (0, other, n1, 1.0)]
    entries += [(1, m0, one, 1.0), (1, m1, one, 1.0), (1, m2, one, 1.0)]
    entries += [(1, one, m0, 1.0), (1, other, m1, 1.0), (2, one, m2, 1.0)]
    out = jnp.zeros((16, 64), f32)
    for block, source, target, value in entries:
        out = jnp.where((r == target) & (c == 16 * block + source), value, out)
    return out.astype(bf16)


def targets_of(feature_rows, mix):
    return lax.dot_general(feature_rows, mix, TN, preferred_element_type=f32).astype(bf16)


def covariance(squared):
    y = jnp.maximum(squared, TINY)
    return jnp.exp2(y * lax.rsqrt(y) * RATE)


def up_body(
    coords_hbm,
    charges_hbm,
    bases_hbm,
    up_hbm,
    top_hbm,
    copies_hbm,
    beside_hbm,
    across_hbm,
    coords,
    charges,
    bases,
    up_transfer,
    top_transfer,
    copies,
    beside,
    across,
    sems,
    group_sems,
):
    leaves = charges.shape[0]
    edge = beside.shape[1]
    group = 4
    small = [
        pltpu.make_async_copy(src, dst, sems.at[k])
        for k, (src, dst) in enumerate(((charges_hbm, charges), (coords_hbm, coords), (top_hbm, top_transfer)))
    ]
    moves = []
    for g in range(leaves // group):
        at = pl.ds(group * g, group)
        moves.append(
            (
                pltpu.make_async_copy(bases_hbm.at[at], bases.at[at], group_sems.at[0, g]),
                pltpu.make_async_copy(up_hbm.at[at], up_transfer.at[at], group_sems.at[1, g]),
            )
        )
    for move in small[0:2] + [m for pair in moves for m in pair] + small[2:]:
        move.start()
    small[0].wait()
    small[1].wait()
    odd = lax.axis_index("leaf") % 2
    sends = []
    for k, (ref, start) in enumerate(((beside, (1 - odd) * (leaves - edge)), (across, odd * (leaves - edge)))):
        start = pl.multiple_of(start, edge)
        for c in range(3):
            ref[c] = coords[c, pl.ds(start, edge), :]
        ref[3] = jnp.zeros(ref.shape[1:], f32)
        for g in range(4):
            ref[4 + g, 0:4, :] = charges[start + 2 * g]
            ref[4 + g, 4:8, :] = charges[start + 2 * g + 1]
        sends.append(pltpu.make_async_copy(ref, (beside_hbm, across_hbm)[k], sems.at[3 + k]))
        sends[k].start()
    mids = []
    lift = None
    for n in range(leaves // 8):
        mid = None
        for g in range(2 * n, 2 * n + 2):
            for move in moves[g]:
                move.wait()
            for leaf in range(group * g, group * g + group):
                coeffs = fold8(dot2(rows8(charges[leaf]), bases[leaf], NT))
                part = fold8(dot2(rows8(coeffs), up_transfer[leaf], NT))
                mid = part if mid is None else mid + part
        mids.append(mid)
        if n == 0:
            small[2].wait()
        part = fold8(dot2(rows8(mid), top_transfer[n], NT))
        lift = part if lift is None else lift + part
    tile = jnp.concatenate(
        [jnp.concatenate(mids, axis=1), jnp.concatenate([lift, jnp.zeros_like(lift)], axis=1)], axis=0
    )
    copies[...] = jnp.broadcast_to(tile, copies.shape)
    sends.append(pltpu.make_async_copy(copies, copies_hbm, sems.at[5]))
    sends[2].start()
    for send in sends:
        send.wait()


def up_call(peers, coords, charges, bases, up_transfer, top_transfer):
    halo = (8, EDGE, coords.shape[2])
    copies = (peers, 8, 128)
    args = (coords, charges, bases, up_transfer, top_transfer)
    return pl.pallas_call(
        up_body,
        out_shape=tuple(jax.ShapeDtypeStruct(shape, f32) for shape in (copies, halo, halo)),
        in_specs=[HBM] * 5,
        out_specs=(HBM, HBM, HBM),
        scratch_shapes=[pltpu.VMEM(a.shape, f32) for a in args]
        + [pltpu.VMEM(shape, f32) for shape in (copies, halo, halo)]
        + [pltpu.SemaphoreType.DMA((6,)), pltpu.SemaphoreType.DMA((2, 4))],
        compiler_params=pltpu.CompilerParams(vmem_limit_bytes=VMEM_LIMIT),
        name="upward",
    )(*args)


def near_body(
    list_hbm,
    count_hbm,
    coords_hbm,
    charges_hbm,
    beside,
    across,
    out,
    near_list,
    near_count,
    coords,
    charges,
    target_rows,
    source_rows,
    source_vals,
    feature_rows,
    square_a,
    square_b,
    kern_a,
    kern_b,
    total_rows,
    pair_t,
    pair_s,
    sems,
    *,
    chunk,
    unroll,
    self_unroll,
    own_unroll,
):
    leaves, _, points = charges.shape
    edge = beside.shape[1]
    slots = near_list.shape[0]
    pairs_of = ((coords_hbm, coords), (list_hbm, near_list), (count_hbm, near_count), (charges_hbm, charges))
    moves = [pltpu.make_async_copy(src, dst, sems.at[k]) for k, (src, dst) in enumerate(pairs_of)]
    for move in moves:
        move.start()
    window_start = lax.axis_index("leaf") * leaves - edge
    odd = lax.axis_index("leaf") % 2
    beside_at = (1 - odd) * (edge + leaves)
    across_at = odd * (edge + leaves)
    mix = mixing()
    for move in moves:
        move.wait()
    total = 0
    for t in range(leaves):
        for j in range(1, slots):
            pair_t[total + j - 1] = t
            pair_s[total + j - 1] = near_list[j, t] - window_start
        total = total + near_count[t] - 1
    for j in range(unroll + 1):
        pair_t[total + j] = leaves
        pair_s[total + j] = 0
    for ref, base, count in ((beside, beside_at, edge), (across, across_at, edge), (coords, edge, leaves)):

        def put(row, value):
            for q in range(points // 128):
                feature_rows.at[q][pl.ds(16 * base + row, count, stride=16), :] = value[:, 128 * q : 128 * q + 128]

        pieces(ref[0], ref[1], ref[2], put)

    def rows_of(slot):
        at = pl.ds(pl.multiple_of(16 * slot, 16), 16)
        rows = jnp.concatenate([feature_rows[q, at, :].astype(bf16) for q in range(points // 128)], axis=1)
        for b in range(4):
            source_rows[slot, 16 * b : 16 * b + 16, :] = rows
        return rows

    def own(i, _):
        target_rows[i] = targets_of(rows_of(edge + i), mix)
        source_vals[edge + i] = rows8(charges[i])
        return 0

    lax.fori_loop(0, leaves, own, 0, unroll=own_unroll)

    def halo(g, _):
        for ref, base in ((beside, beside_at), (across, across_at)):
            for k in range(2):
                rows_of(base + 2 * g + k)
                source_vals[base + 2 * g + k] = rows8(ref[4 + g, 4 * k : 4 * k + 4, :])
        return 0

    lax.fori_loop(0, edge // 2, halo, 0)

    def distances(i, dst, c):
        dst[c : c + chunk, :] = jnp.dot(
            target_rows[pair_t[i], c : c + chunk, :], source_rows[pair_s[i]], preferred_element_type=f32
        )

    def kernels(src, dst, c):
        high, low = split2(covariance(src[c : c + chunk, :]))
        dst[0, c : c + chunk, :] = high
        dst[1, c : c + chunk, :] = low

    def apply(i, src, c):
        vals = source_vals[pair_s[i]]
        total_rows[pair_t[i], :, c : c + chunk] += lax.dot_general(
            vals, src[0, c : c + chunk, :], NT, preferred_element_type=f32
        ) + lax.dot_general(vals, src[1, c : c + chunk, :], NT, preferred_element_type=f32)

    def self_distances(t, dst, c):
        rows = slice(c, c + BLOCK)
        dst[rows, c:] = jnp.dot(target_rows[t, rows, :], source_rows[edge + t, :, c:], preferred_element_type=f32)

    def self_kernels(src, dst, c):
        high, low = split2(covariance(src[c : c + BLOCK, c:]))
        dst[0, c : c + BLOCK, c:] = high
        dst[1, c : c + BLOCK, c:] = low

    def self_apply(t, src):
        vals = source_vals[edge + t]
        sums = []
        for c in blocks:
            part = None
            for p in range(2):
                term = lax.dot_general(vals[:, c:], src[p, c : c + BLOCK, c:], NT, preferred_element_type=f32)
                part = term if part is None else part + term
                if c:
                    part += jnp.dot(vals[:, :c], src[p, :c, c : c + BLOCK], preferred_element_type=f32)
            sums.append(part)
        total_rows[t] = jnp.concatenate(sums, axis=1)

    blocks = range(0, points, BLOCK)
    for c in blocks:
        self_distances(0, square_a, c)

    def self_step(k, _):
        i = self_unroll * k
        for u in range(0, self_unroll, 2):
            for c in blocks:
                self_kernels(square_a, kern_a, c)
                self_distances(i + u + 1, square_b, c)
            self_apply(jnp.where(k == 0, leaves, i - 1) if u == 0 else i + u - 1, kern_b)
            for c in blocks:
                self_kernels(square_b, kern_b, c)
                self_distances(i + u + 2, square_a, c)
            self_apply(i + u, kern_a)
        return 0

    lax.fori_loop(0, leaves // self_unroll, self_step, 0)
    chunks = range(0, points, chunk)
    for c in chunks:
        distances(0, square_a, c)
    self_apply(leaves - 1, kern_b)

    def step(k, _):
        i = unroll * k
        previous = jnp.where(k == 0, total, i - 1)
        for u in range(0, unroll, 2):
            for c in chunks:
                kernels(square_a, kern_a, c)
                distances(i + u + 1, square_b, c)
                apply(previous if u == 0 else i + u - 1, kern_b, c)
            for c in chunks:
                kernels(square_b, kern_b, c)
                distances(i + u + 2, square_a, c)
                apply(i + u, kern_a, c)
        return 0

    trips = (total + unroll - 1) // unroll
    lax.fori_loop(0, trips, step, 0)
    for c in chunks:
        apply(jnp.maximum(unroll * trips - 1, 0), kern_b, c)

    def finish(i, _):
        out[i] = fold8(total_rows[i])
        return 0

    lax.fori_loop(0, leaves, finish, 0, unroll=4)


def near_call(near_list, near_count, coords, charges, beside, across, chunk=128, unroll=2, self_unroll=2, own_unroll=4):
    leaves, _, points = charges.shape
    window = leaves + 2 * EDGE
    pairs = near_list.shape[0] * leaves + unroll + 4
    return pl.pallas_call(
        functools.partial(near_body, chunk=chunk, unroll=unroll, self_unroll=self_unroll, own_unroll=own_unroll),
        out_shape=jax.ShapeDtypeStruct((leaves, NRHS, points), f32),
        in_specs=[HBM] * 4 + [VM] * 2,
        out_specs=VM,
        scratch_shapes=[
            pltpu.SMEM(near_list.shape, jnp.int32),
            pltpu.SMEM(near_count.shape, jnp.int32),
            pltpu.VMEM(coords.shape, f32),
            pltpu.VMEM(charges.shape, f32),
            pltpu.VMEM((leaves + 1, points, 64), bf16),
            pltpu.VMEM((window, 64, points), bf16),
            pltpu.VMEM((window, 2 * NRHS, points), bf16),
            pltpu.VMEM((points // 128, window * 16, 128), f32),
            pltpu.VMEM((points, points), f32),
            pltpu.VMEM((points, points), f32),
            pltpu.VMEM((2, points, points), bf16),
            pltpu.VMEM((2, points, points), bf16),
            pltpu.VMEM((leaves + 1, 2 * NRHS, points), f32),
            pltpu.SMEM((pairs,), jnp.int32),
            pltpu.SMEM((pairs,), jnp.int32),
            pltpu.SemaphoreType.DMA((4,)),
        ],
        compiler_params=pltpu.CompilerParams(vmem_limit_bytes=VMEM_LIMIT),
        name="near",
    )(near_list, near_count, coords, charges, beside, across)


def far_body(
    far_mid_hbm,
    mid_count_hbm,
    far_top_hbm,
    top_count_hbm,
    proxy_mid_hbm,
    proxy_top_hbm,
    top_hbm,
    up_hbm,
    bases_hbm,
    gathered_hbm,
    near_hbm,
    out,
    far_mid,
    mid_count,
    far_top,
    top_count,
    proxy_mid,
    proxy_top,
    top_transfer,
    up_transfer,
    bases,
    gathered,
    near,
    mid_points,
    top_points,
    pts,
    coef,
    kern,
    sems,
):
    sources = (
        far_mid_hbm,
        mid_count_hbm,
        far_top_hbm,
        top_count_hbm,
        proxy_mid_hbm,
        proxy_top_hbm,
        gathered_hbm,
        top_hbm,
        up_hbm,
        bases_hbm,
        near_hbm,
    )
    inputs = (far_mid, mid_count, far_top, top_count, proxy_mid, proxy_top)
    places = inputs + (gathered, top_transfer, up_transfer, bases, near)
    moves = [pltpu.make_async_copy(src, dst, sems.at[k]) for k, (src, dst) in enumerate(zip(sources, places))]
    for move in moves:
        move.start()
    leaves = near.shape[0]
    nodes = leaves // 8
    rank = bases.shape[1]
    device = lax.axis_index("leaf")
    own = device * nodes
    parent = own // 8
    mix = mixing()
    for move in moves[0:6]:
        move.wait()
    for k in range(3):
        mids, tops = proxy_mid[k].T, proxy_top[k]
        mid_points[pl.ds(k, mids.shape[0], stride=4), :] = jnp.concatenate([mids, mids], axis=1)
        top_points[pl.ds(k, tops.shape[0], stride=4), :] = jnp.concatenate([tops, tops], axis=1)

    def proxy(ref, node):
        return ref[pl.ds(4 * node, 3), :]

    lane = lax.broadcasted_iota(jnp.int32, (NRHS, 2 * rank), 1)

    def kernels_of(k, node, ids, nodes_points):
        slots = ids.shape[0]
        width = rank * slots
        for j in range(0, slots, 2):
            a, b = ids[j, node], ids[j + 1, node]
            pts[k, 0:3, rank * j : rank * j + 2 * rank] = jnp.where(
                lane[0:3] < rank, proxy(nodes_points, a), proxy(nodes_points, b)
            )
        rows = features(pts[k, 0:3, 0:width])
        squared = jnp.dot(
            targets_of(features(proxy(nodes_points, node)[:, 0:rank]), mix),
            jnp.concatenate([rows] * 4, axis=0),
            preferred_element_type=f32,
        )
        high, low = split2(covariance(squared))
        kern[k, 0, :, 0:width] = high
        kern[k, 1, :, 0:width] = low

    def field(k, node, ids, count, coeffs_of):
        slots = ids.shape[0]
        width = rank * slots
        for j in range(0, slots, 2):
            left = jnp.where(j < count, coeffs_of(ids[j, node], 0), 0.0)
            right = jnp.where(j + 1 < count, coeffs_of(ids[j + 1, node], 1), 0.0)
            coef[k, :, rank * j : rank * j + 2 * rank] = jnp.where(lane < rank, left, right)
        vals = rows8(coef[k, :, 0:width])
        return fold8(
            lax.dot_general(vals, kern[k, 0, :, 0:width], NT, preferred_element_type=f32)
            + lax.dot_general(vals, kern[k, 1, :, 0:width], NT, preferred_element_type=f32)
        )

    def mid_coeffs(s, half):
        node = gathered[lax.shift_right_logical(s, 1), 0:NRHS, :]
        return jnp.where((s & 1) == half, node, pltpu.roll(node, rank, 1))

    def top_coeffs(s, half):
        node = gathered[4 * s, NRHS : 2 * NRHS, :]
        for k in range(1, 4):
            node = node + gathered[4 * s + k, NRHS : 2 * NRHS, :]
        return node if half == 0 else pltpu.roll(node, rank, 1)

    kernels_of(nodes, parent, far_top, top_points)
    for n in range(nodes):
        kernels_of(n, own + n, far_mid, mid_points)
    for move in moves[6:]:
        move.wait()
    top8 = rows8(field(nodes, parent, far_top, top_count[parent], top_coeffs))
    for n in range(nodes):
        mid_field = field(n, own + n, far_mid, mid_count[own + n], mid_coeffs)
        mid_field = mid_field + fold8(dot2(top8, top_transfer[n], (((1,), (0,)), ((), ()))))
        mid8 = rows8(mid_field)
        for leaf in range(8 * n, 8 * n + 8):
            leaf_field = fold8(dot2(mid8, up_transfer[leaf], (((1,), (0,)), ((), ()))))
            far = fold8(dot2(rows8(leaf_field), bases[leaf], (((1,), (0,)), ((), ()))))
            out[leaf] = (near[leaf] + far) * out_scale


def far_call(
    far_mid, mid_count, far_top, top_count, proxy_mid, proxy_top, top_transfer, up_transfer, bases, gathered, near
):
    width = bases.shape[1] * max(far_mid.shape[0], far_top.shape[0])
    integers = (far_mid, mid_count, far_top, top_count)
    floats = (proxy_mid, proxy_top, top_transfer, up_transfer, bases, gathered, near)
    fields = near.shape[0] // 8 + 1
    return pl.pallas_call(
        far_body,
        out_shape=jax.ShapeDtypeStruct(near.shape, f32),
        in_specs=[HBM] * 11,
        out_specs=VM,
        scratch_shapes=[pltpu.SMEM(a.shape, jnp.int32) for a in integers]
        + [pltpu.VMEM(a.shape, f32) for a in floats]
        + [
            pltpu.VMEM((4 * proxy_mid.shape[2], 2 * proxy_mid.shape[1]), f32),
            pltpu.VMEM((4 * proxy_top.shape[1], 2 * proxy_top.shape[2]), f32),
            pltpu.VMEM((fields, 8, width), f32),
            pltpu.VMEM((fields, NRHS, width), f32),
            pltpu.VMEM((fields, 2, bases.shape[1], width), bf16),
            pltpu.SemaphoreType.DMA((11,)),
        ],
        compiler_params=pltpu.CompilerParams(vmem_limit_bytes=VMEM_LIMIT),
        name="far",
    )(*integers, *floats)


def shards(
    coords,
    charges,
    bases,
    up_transfer,
    top_transfer,
    proxy_mid,
    proxy_top,
    near_list,
    near_count,
    far_mid,
    far_mid_count,
    far_top,
    far_top_count,
):
    peers = lax.axis_size("leaf")
    chip = [(i, i ^ 1) for i in range(peers)]
    next_chip = [(i, i + 1 if i % 2 else i - 1) for i in range(1, peers - 1)]
    coords = jnp.transpose(coords, (1, 0, 2))
    copies, beside, across = up_call(peers, coords, charges, bases, up_transfer, top_transfer)
    across = lax.ppermute(across, "leaf", next_chip)
    beside = lax.ppermute(beside, "leaf", chip)
    gathered = lax.all_to_all(copies, "leaf", 0, 0, tiled=True)
    near = near_call(near_list.T, near_count, coords, charges, beside, across)
    return far_call(
        far_mid.T,
        far_mid_count,
        far_top.T,
        far_top_count,
        jnp.transpose(proxy_mid, (1, 2, 0)),
        jnp.transpose(proxy_top, (1, 0, 2)),
        top_transfer,
        up_transfer,
        bases,
        gathered,
        near,
    )


def solution(mesh):
    placed = (
        P("leaf", None, None),
        P("leaf", None, None),
        P("leaf", None, None),
        P("leaf", None, None),
        P("leaf", None, None),
        P(),
        P(),
        P("leaf", None),
        P("leaf"),
        P(),
        P(),
        P(),
        P(),
    )
    return jax.shard_map(
        shards, mesh=mesh, in_specs=placed, out_specs=P("leaf", None, None), check_vma=False
    )
```

```python
import functools

import jax
import jax.numpy as jnp
from jax import lax
from jax.experimental import pallas as pl
from jax.experimental.pallas import tpu as pltpu
from jax.sharding import PartitionSpec as P


EDGE = 8
NRHS = 4
length_scale = 0.4
out_scale = 0.125
TINY = 1e-30
RATE = -1.4426950408889634 / length_scale
NT = (((1,), (1,)), ((), ()))
TN = (((0,), (0,)), ((), ()))
bf16 = jnp.bfloat16
f32 = jnp.float32
VM = pl.BlockSpec(memory_space=pltpu.VMEM)
HBM = pl.BlockSpec(memory_space=pltpu.HBM)
VMEM_LIMIT = 67043328
BLOCK = 128


def snap(value, magic):
    return (value + magic) - magic


def split2(value):
    high = value.astype(bf16)
    return high, (value - high.astype(f32)).astype(bf16)


def rows8(value):
    high, low = split2(value)
    return jnp.concatenate([high.astype(f32), low.astype(f32)], axis=0).astype(bf16)


def fold8(value):
    return value[0:NRHS] + value[NRHS : 2 * NRHS]


def dot2(rows, value, dims):
    high, low = split2(value)
    return lax.dot_general(rows, high, dims, preferred_element_type=f32) + lax.dot_general(
        rows, low, dims, preferred_element_type=f32
    )


def pieces(x0, x1, x2, put):
    n = m = None
    for k, points in enumerate((x0, x1, x2)):
        x = points - 0.5
        h = snap(x, 49152.0)
        low = x - h
        l0 = snap(low, 96.0)
        put(k, h)
        put(8 + k, l0)
        put(11 + k, low - l0)
        n = h * h if n is None else n + h * h
        part = low * (h + h + low)
        m = part if m is None else m + part
    n0 = snap(n, 49152.0)
    m0 = snap(m, 384.0)
    m1 = snap(m - m0, 1.5)
    for row, value in ((3, n0), (4, n - n0), (7, m0), (14, m1), (15, m - m0 - m1)):
        put(row, value)
    one = jnp.ones_like(n)
    put(5, one)
    put(6, one)


def features(points):
    rows = [None] * 16

    def put(row, value):
        rows[row] = value

    pieces(points[0:1], points[1:2], points[2:3], put)
    return jnp.concatenate(rows, axis=0).astype(bf16)


def mixing():
    r = lax.broadcasted_iota(jnp.int32, (16, 64), 0)
    c = lax.broadcasted_iota(jnp.int32, (16, 64), 1)
    h, l0, l1 = (0, 1, 2), (8, 9, 10), (11, 12, 13)
    n0, n1, one, other, m0, m1, m2 = 3, 4, 5, 6, 7, 14, 15
    entries = []
    for k in range(3):
        entries += [(0, h[k], h[k], -2.0)]
        entries += [(1, h[k], l0[k], -2.0), (1, l0[k], h[k], -2.0), (1, l1[k], h[k], -2.0)]
        entries += [(2, h[k], l1[k], -2.0), (2, l0[k], l0[k], -2.0), (2, l1[k], l0[k], -2.0)]
        entries += [(3, l0[k], l1[k], -2.0), (3, l1[k], l1[k], -2.0)]
    entries += [(0, n0, one, 1.0), (0, n1, one, 1.0), (0, one, n0, 1.0), (0, other, n1, 1.0)]
    entries += [(1, m0, one, 1.0), (1, m1, one, 1.0), (1, m2, one, 1.0)]
    entries += [(1, one, m0, 1.0), (1, other, m1, 1.0), (2, one, m2, 1.0)]
    out = jnp.zeros((16, 64), f32)
    for block, source, target, value in entries:
        out = jnp.where((r == target) & (c == 16 * block + source), value, out)
    return out.astype(bf16)


def targets_of(feature_rows, mix):
    return lax.dot_general(feature_rows, mix, TN, preferred_element_type=f32).astype(bf16)


def covariance(squared):
    y = jnp.maximum(squared, TINY)
    return jnp.exp2(y * lax.rsqrt(y) * RATE)


def spread(ref, base, count, feature_rows):
    def put(row, value):
        for q in range(feature_rows.shape[0]):
            feature_rows.at[q][pl.ds(16 * base + row, count, stride=16), :] = value[:, 128 * q : 128 * q + 128]

    pieces(ref[0], ref[1], ref[2], put)


def source_of(slot, feature_rows, source_rows):
    at = pl.ds(pl.multiple_of(16 * slot, 16), 16)
    rows = jnp.concatenate([feature_rows[q, at, :].astype(bf16) for q in range(feature_rows.shape[0])], axis=1)
    for b in range(4):
        source_rows[slot, 16 * b : 16 * b + 16, :] = rows
    return rows


def up_body(
    coords_hbm,
    charges_hbm,
    bases_hbm,
    up_hbm,
    top_hbm,
    copies_hbm,
    beside_hbm,
    across_hbm,
    self_hbm,
    coords,
    charges,
    bases,
    up_transfer,
    top_transfer,
    copies,
    beside,
    across,
    self_part,
    target_rows,
    source_rows,
    source_vals,
    feature_rows,
    square_a,
    square_b,
    kern_a,
    kern_b,
    total_rows,
    sems,
    group_sems,
    *,
    self_unroll,
):
    leaves, _, points = charges.shape
    edge = beside.shape[1]
    group = 4
    mix = mixing()
    small = [
        pltpu.make_async_copy(src, dst, sems.at[k])
        for k, (src, dst) in enumerate(((charges_hbm, charges), (coords_hbm, coords), (top_hbm, top_transfer)))
    ]
    moves = []
    for g in range(leaves // group):
        at = pl.ds(group * g, group)
        moves.append(
            (
                pltpu.make_async_copy(bases_hbm.at[at], bases.at[at], group_sems.at[0, g]),
                pltpu.make_async_copy(up_hbm.at[at], up_transfer.at[at], group_sems.at[1, g]),
            )
        )
    for move in small[0:2] + [m for pair in moves for m in pair] + small[2:]:
        move.start()
    small[0].wait()
    small[1].wait()
    odd = lax.axis_index("leaf") % 2
    sends = []
    for k, (ref, start) in enumerate(((beside, (1 - odd) * (leaves - edge)), (across, odd * (leaves - edge)))):
        start = pl.multiple_of(start, edge)
        for c in range(3):
            ref[c] = coords[c, pl.ds(start, edge), :]
        ref[3] = jnp.zeros(ref.shape[1:], f32)
        for g in range(4):
            ref[4 + g, 0:4, :] = charges[start + 2 * g]
            ref[4 + g, 4:8, :] = charges[start + 2 * g + 1]
        sends.append(pltpu.make_async_copy(ref, (beside_hbm, across_hbm)[k], sems.at[3 + k]))
        sends[k].start()
    spread(coords, 0, leaves, feature_rows)

    def own(i, _):
        target_rows[i] = targets_of(source_of(i, feature_rows, source_rows), mix)
        source_vals[i] = rows8(charges[i])
        return 0

    lax.fori_loop(0, leaves, own, 0, unroll=4)

    def self_distances(t, dst, c):
        rows = slice(c, c + BLOCK)
        dst[rows, c:] = jnp.dot(target_rows[t, rows, :], source_rows[t, :, c:], preferred_element_type=f32)

    def self_kernels(src, dst, c):
        high, low = split2(covariance(src[c : c + BLOCK, c:]))
        dst[0, c : c + BLOCK, c:] = high
        dst[1, c : c + BLOCK, c:] = low

    def self_apply(t, src):
        vals = source_vals[t]
        sums = []
        for c in blocks:
            part = None
            for p in range(2):
                term = lax.dot_general(vals[:, c:], src[p, c : c + BLOCK, c:], NT, preferred_element_type=f32)
                part = term if part is None else part + term
                if c:
                    part += jnp.dot(vals[:, :c], src[p, :c, c : c + BLOCK], preferred_element_type=f32)
            sums.append(part)
        total_rows[t] = jnp.concatenate(sums, axis=1)

    blocks = range(0, points, BLOCK)
    for c in blocks:
        self_distances(0, square_a, c)

    def self_step(k, _):
        i = self_unroll * k
        for u in range(0, self_unroll, 2):
            for c in blocks:
                self_kernels(square_a, kern_a, c)
                self_distances(i + u + 1, square_b, c)
            self_apply(jnp.where(k == 0, leaves, i - 1) if u == 0 else i + u - 1, kern_b)
            for c in blocks:
                self_kernels(square_b, kern_b, c)
                self_distances(i + u + 2, square_a, c)
            self_apply(i + u, kern_a)
        return 0

    lax.fori_loop(0, leaves // self_unroll, self_step, 0)
    self_apply(leaves - 1, kern_b)

    for leaf in range(leaves):
        self_part[leaf] = fold8(total_rows[leaf])
    sends.append(pltpu.make_async_copy(self_part, self_hbm, sems.at[6]))
    sends[2].start()
    mids = []
    lift = None
    for n in range(leaves // 8):
        mid = None
        for g in range(2 * n, 2 * n + 2):
            for move in moves[g]:
                move.wait()
            for leaf in range(group * g, group * g + group):
                coeffs = fold8(dot2(rows8(charges[leaf]), bases[leaf], NT))
                part = fold8(dot2(rows8(coeffs), up_transfer[leaf], NT))
                mid = part if mid is None else mid + part
        mids.append(mid)
        if n == 0:
            small[2].wait()
        part = fold8(dot2(rows8(mid), top_transfer[n], NT))
        lift = part if lift is None else lift + part
    tile = jnp.concatenate(
        [jnp.concatenate(mids, axis=1), jnp.concatenate([lift, jnp.zeros_like(lift)], axis=1)], axis=0
    )
    copies[...] = jnp.broadcast_to(tile, copies.shape)
    sends.append(pltpu.make_async_copy(copies, copies_hbm, sems.at[5]))
    sends[3].start()
    for send in sends:
        send.wait()


def up_call(peers, coords, charges, bases, up_transfer, top_transfer, self_unroll=2):
    leaves, _, points = charges.shape
    halo = (8, EDGE, points)
    copies = (peers, 8, 128)
    args = (coords, charges, bases, up_transfer, top_transfer)
    return pl.pallas_call(
        functools.partial(up_body, self_unroll=self_unroll),
        out_shape=tuple(jax.ShapeDtypeStruct(shape, f32) for shape in (copies, halo, halo, charges.shape)),
        in_specs=[HBM] * 5,
        out_specs=(HBM,) * 4,
        scratch_shapes=[pltpu.VMEM(a.shape, f32) for a in args]
        + [pltpu.VMEM(shape, f32) for shape in (copies, halo, halo, charges.shape)]
        + [
            pltpu.VMEM((leaves + 1, points, 64), bf16),
            pltpu.VMEM((leaves + 1, 64, points), bf16),
            pltpu.VMEM((leaves + 1, 2 * NRHS, points), bf16),
            pltpu.VMEM((points // 128, leaves * 16, 128), f32),
            pltpu.VMEM((points, points), f32),
            pltpu.VMEM((points, points), f32),
            pltpu.VMEM((2, points, points), bf16),
            pltpu.VMEM((2, points, points), bf16),
            pltpu.VMEM((leaves + 1, 2 * NRHS, points), f32),
        ]
        + [pltpu.SemaphoreType.DMA((7,)), pltpu.SemaphoreType.DMA((2, 4))],
        compiler_params=pltpu.CompilerParams(vmem_limit_bytes=VMEM_LIMIT),
        name="upward",
    )(*args)


def near_body(
    list_hbm,
    count_hbm,
    coords_hbm,
    charges_hbm,
    self_hbm,
    beside,
    across,
    out,
    near_list,
    near_count,
    coords,
    charges,
    self_part,
    target_rows,
    source_rows,
    source_vals,
    feature_rows,
    square_a,
    square_b,
    kern_a,
    kern_b,
    total_rows,
    pair_t,
    pair_s,
    sems,
    *,
    chunk,
    unroll,
    own_unroll,
):
    leaves, _, points = charges.shape
    edge = beside.shape[1]
    slots = near_list.shape[0]
    pairs_of = ((coords_hbm, coords), (list_hbm, near_list), (count_hbm, near_count), (charges_hbm, charges))
    pairs_of += ((self_hbm, self_part),)
    moves = [pltpu.make_async_copy(src, dst, sems.at[k]) for k, (src, dst) in enumerate(pairs_of)]
    for move in moves:
        move.start()
    window_start = lax.axis_index("leaf") * leaves - edge
    odd = lax.axis_index("leaf") % 2
    beside_at = (1 - odd) * (edge + leaves)
    across_at = odd * (edge + leaves)
    mix = mixing()
    total_rows[...] = jnp.zeros_like(total_rows)
    for move in moves:
        move.wait()
    total = 0
    for t in range(leaves):
        for j in range(1, slots):
            pair_t[total + j - 1] = t
            pair_s[total + j - 1] = near_list[j, t] - window_start
        total = total + near_count[t] - 1
    for j in range(unroll + 1):
        pair_t[total + j] = leaves
        pair_s[total + j] = 0
    for ref, base, count in ((beside, beside_at, edge), (across, across_at, edge), (coords, edge, leaves)):

        spread(ref, base, count, feature_rows)

    def own(i, _):
        target_rows[i] = targets_of(source_of(edge + i, feature_rows, source_rows), mix)
        source_vals[edge + i] = rows8(charges[i])
        return 0

    lax.fori_loop(0, leaves, own, 0, unroll=own_unroll)

    def halo(g, _):
        for ref, base in ((beside, beside_at), (across, across_at)):
            for k in range(2):
                source_of(base + 2 * g + k, feature_rows, source_rows)
                source_vals[base + 2 * g + k] = rows8(ref[4 + g, 4 * k : 4 * k + 4, :])
        return 0

    lax.fori_loop(0, edge // 2, halo, 0)

    def distances(i, dst, c):
        dst[c : c + chunk, :] = jnp.dot(
            target_rows[pair_t[i], c : c + chunk, :], source_rows[pair_s[i]], preferred_element_type=f32
        )

    def kernels(src, dst, c):
        high, low = split2(covariance(src[c : c + chunk, :]))
        dst[0, c : c + chunk, :] = high
        dst[1, c : c + chunk, :] = low

    def apply(i, src, c):
        vals = source_vals[pair_s[i]]
        total_rows[pair_t[i], :, c : c + chunk] += lax.dot_general(
            vals, src[0, c : c + chunk, :], NT, preferred_element_type=f32
        ) + lax.dot_general(vals, src[1, c : c + chunk, :], NT, preferred_element_type=f32)

    chunks = range(0, points, chunk)
    for c in chunks:
        distances(0, square_a, c)

    def step(k, _):
        i = unroll * k
        previous = jnp.where(k == 0, total, i - 1)
        for u in range(0, unroll, 2):
            for c in chunks:
                kernels(square_a, kern_a, c)
                distances(i + u + 1, square_b, c)
                apply(previous if u == 0 else i + u - 1, kern_b, c)
            for c in chunks:
                kernels(square_b, kern_b, c)
                distances(i + u + 2, square_a, c)
                apply(i + u, kern_a, c)
        return 0

    trips = (total + unroll - 1) // unroll
    lax.fori_loop(0, trips, step, 0)
    for c in chunks:
        apply(jnp.maximum(unroll * trips - 1, 0), kern_b, c)

    def finish(i, _):
        out[i] = fold8(total_rows[i]) + self_part[i]
        return 0

    lax.fori_loop(0, leaves, finish, 0, unroll=4)


def near_call(near_list, near_count, coords, charges, self_part, beside, across, chunk=128, unroll=4, own_unroll=4):
    leaves, _, points = charges.shape
    window = leaves + 2 * EDGE
    pairs = near_list.shape[0] * leaves + unroll + 4
    return pl.pallas_call(
        functools.partial(near_body, chunk=chunk, unroll=unroll, own_unroll=own_unroll),
        out_shape=jax.ShapeDtypeStruct((leaves, NRHS, points), f32),
        in_specs=[HBM] * 5 + [VM] * 2,
        out_specs=VM,
        scratch_shapes=[
            pltpu.SMEM(near_list.shape, jnp.int32),
            pltpu.SMEM(near_count.shape, jnp.int32),
            pltpu.VMEM(coords.shape, f32),
            pltpu.VMEM(charges.shape, f32),
            pltpu.VMEM(charges.shape, f32),
            pltpu.VMEM((leaves + 1, points, 64), bf16),
            pltpu.VMEM((window, 64, points), bf16),
            pltpu.VMEM((window, 2 * NRHS, points), bf16),
            pltpu.VMEM((points // 128, window * 16, 128), f32),
            pltpu.VMEM((points, points), f32),
            pltpu.VMEM((points, points), f32),
            pltpu.VMEM((2, points, points), bf16),
            pltpu.VMEM((2, points, points), bf16),
            pltpu.VMEM((leaves + 1, 2 * NRHS, points), f32),
            pltpu.SMEM((pairs,), jnp.int32),
            pltpu.SMEM((pairs,), jnp.int32),
            pltpu.SemaphoreType.DMA((5,)),
        ],
        compiler_params=pltpu.CompilerParams(vmem_limit_bytes=VMEM_LIMIT),
        name="near",
    )(near_list, near_count, coords, charges, self_part, beside, across)


def far_body(
    far_mid_hbm,
    mid_count_hbm,
    far_top_hbm,
    top_count_hbm,
    proxy_mid_hbm,
    proxy_top_hbm,
    top_hbm,
    up_hbm,
    bases_hbm,
    gathered_hbm,
    near_hbm,
    out,
    far_mid,
    mid_count,
    far_top,
    top_count,
    proxy_mid,
    proxy_top,
    top_transfer,
    up_transfer,
    bases,
    gathered,
    near,
    mid_points,
    top_points,
    pts,
    coef,
    kern,
    sems,
):
    sources = (
        far_mid_hbm,
        mid_count_hbm,
        far_top_hbm,
        top_count_hbm,
        proxy_mid_hbm,
        proxy_top_hbm,
        gathered_hbm,
        top_hbm,
        up_hbm,
        bases_hbm,
        near_hbm,
    )
    inputs = (far_mid, mid_count, far_top, top_count, proxy_mid, proxy_top)
    places = inputs + (gathered, top_transfer, up_transfer, bases, near)
    moves = [pltpu.make_async_copy(src, dst, sems.at[k]) for k, (src, dst) in enumerate(zip(sources, places))]
    for move in moves:
        move.start()
    leaves = near.shape[0]
    nodes = leaves // 8
    rank = bases.shape[1]
    device = lax.axis_index("leaf")
    own = device * nodes
    parent = own // 8
    mix = mixing()
    for move in moves[0:6]:
        move.wait()
    for k in range(3):
        mids, tops = proxy_mid[k].T, proxy_top[k]
        mid_points[pl.ds(k, mids.shape[0], stride=4), :] = jnp.concatenate([mids, mids], axis=1)
        top_points[pl.ds(k, tops.shape[0], stride=4), :] = jnp.concatenate([tops, tops], axis=1)

    def proxy(ref, node):
        return ref[pl.ds(4 * node, 3), :]

    lane = lax.broadcasted_iota(jnp.int32, (NRHS, 2 * rank), 1)

    def kernels_of(k, node, ids, nodes_points):
        slots = ids.shape[0]
        width = rank * slots
        for j in range(0, slots, 2):
            a, b = ids[j, node], ids[j + 1, node]
            pts[k, 0:3, rank * j : rank * j + 2 * rank] = jnp.where(
                lane[0:3] < rank, proxy(nodes_points, a), proxy(nodes_points, b)
            )
        rows = features(pts[k, 0:3, 0:width])
        squared = jnp.dot(
            targets_of(features(proxy(nodes_points, node)[:, 0:rank]), mix),
            jnp.concatenate([rows] * 4, axis=0),
            preferred_element_type=f32,
        )
        high, low = split2(covariance(squared))
        kern[k, 0, :, 0:width] = high
        kern[k, 1, :, 0:width] = low

    def field(k, node, ids, count, coeffs_of):
        slots = ids.shape[0]
        width = rank * slots
        for j in range(0, slots, 2):
            left = jnp.where(j < count, coeffs_of(ids[j, node], 0), 0.0)
            right = jnp.where(j + 1 < count, coeffs_of(ids[j + 1, node], 1), 0.0)
            coef[k, :, rank * j : rank * j + 2 * rank] = jnp.where(lane < rank, left, right)
        vals = rows8(coef[k, :, 0:width])
        return fold8(
            lax.dot_general(vals, kern[k, 0, :, 0:width], NT, preferred_element_type=f32)
            + lax.dot_general(vals, kern[k, 1, :, 0:width], NT, preferred_element_type=f32)
        )

    def mid_coeffs(s, half):
        node = gathered[lax.shift_right_logical(s, 1), 0:NRHS, :]
        return jnp.where((s & 1) == half, node, pltpu.roll(node, rank, 1))

    def top_coeffs(s, half):
        node = gathered[4 * s, NRHS : 2 * NRHS, :]
        for k in range(1, 4):
            node = node + gathered[4 * s + k, NRHS : 2 * NRHS, :]
        return node if half == 0 else pltpu.roll(node, rank, 1)

    kernels_of(nodes, parent, far_top, top_points)
    for n in range(nodes):
        kernels_of(n, own + n, far_mid, mid_points)
    for move in moves[6:]:
        move.wait()
    top8 = rows8(field(nodes, parent, far_top, top_count[parent], top_coeffs))
    for n in range(nodes):
        mid_field = field(n, own + n, far_mid, mid_count[own + n], mid_coeffs)
        mid_field = mid_field + fold8(dot2(top8, top_transfer[n], (((1,), (0,)), ((), ()))))
        mid8 = rows8(mid_field)
        for leaf in range(8 * n, 8 * n + 8):
            leaf_field = fold8(dot2(mid8, up_transfer[leaf], (((1,), (0,)), ((), ()))))
            far = fold8(dot2(rows8(leaf_field), bases[leaf], (((1,), (0,)), ((), ()))))
            out[leaf] = (near[leaf] + far) * out_scale


def far_call(
    far_mid, mid_count, far_top, top_count, proxy_mid, proxy_top, top_transfer, up_transfer, bases, gathered, near
):
    width = bases.shape[1] * max(far_mid.shape[0], far_top.shape[0])
    integers = (far_mid, mid_count, far_top, top_count)
    floats = (proxy_mid, proxy_top, top_transfer, up_transfer, bases, gathered, near)
    fields = near.shape[0] // 8 + 1
    return pl.pallas_call(
        far_body,
        out_shape=jax.ShapeDtypeStruct(near.shape, f32),
        in_specs=[HBM] * 11,
        out_specs=VM,
        scratch_shapes=[pltpu.SMEM(a.shape, jnp.int32) for a in integers]
        + [pltpu.VMEM(a.shape, f32) for a in floats]
        + [
            pltpu.VMEM((4 * proxy_mid.shape[2], 2 * proxy_mid.shape[1]), f32),
            pltpu.VMEM((4 * proxy_top.shape[1], 2 * proxy_top.shape[2]), f32),
            pltpu.VMEM((fields, 8, width), f32),
            pltpu.VMEM((fields, NRHS, width), f32),
            pltpu.VMEM((fields, 2, bases.shape[1], width), bf16),
            pltpu.SemaphoreType.DMA((11,)),
        ],
        compiler_params=pltpu.CompilerParams(vmem_limit_bytes=VMEM_LIMIT),
        name="far",
    )(*integers, *floats)


def shards(
    coords,
    charges,
    bases,
    up_transfer,
    top_transfer,
    proxy_mid,
    proxy_top,
    near_list,
    near_count,
    far_mid,
    far_mid_count,
    far_top,
    far_top_count,
):
    peers = lax.axis_size("leaf")
    chip = [(i, i ^ 1) for i in range(peers)]
    next_chip = [(i, i + 1 if i % 2 else i - 1) for i in range(1, peers - 1)]
    coords = jnp.transpose(coords, (1, 0, 2))
    copies, beside, across, self_part = up_call(peers, coords, charges, bases, up_transfer, top_transfer)
    across = lax.ppermute(across, "leaf", next_chip)
    beside = lax.ppermute(beside, "leaf", chip)
    gathered = lax.all_to_all(copies, "leaf", 0, 0, tiled=True)
    near = near_call(near_list.T, near_count, coords, charges, self_part, beside, across)
    return far_call(
        far_mid.T,
        far_mid_count,
        far_top.T,
        far_top_count,
        jnp.transpose(proxy_mid, (1, 2, 0)),
        jnp.transpose(proxy_top, (1, 0, 2)),
        top_transfer,
        up_transfer,
        bases,
        gathered,
        near,
    )


def solution(mesh):
    placed = (
        P("leaf", None, None),
        P("leaf", None, None),
        P("leaf", None, None),
        P("leaf", None, None),
        P("leaf", None, None),
        P(),
        P(),
        P("leaf", None),
        P("leaf"),
        P(),
        P(),
        P(),
        P(),
    )
    return jax.shard_map(
        shards, mesh=mesh, in_specs=placed, out_specs=P("leaf", None, None), check_vma=False
    )
```

```python
import functools

import jax
import jax.numpy as jnp
from jax import lax
from jax.experimental import pallas as pl
from jax.experimental.pallas import tpu as pltpu
from jax.sharding import PartitionSpec as P


EDGE = 8
NRHS = 4
length_scale = 0.4
out_scale = 0.125
TINY = 1e-30
RATE = -1.4426950408889634 / length_scale
NT = (((1,), (1,)), ((), ()))
TN = (((0,), (0,)), ((), ()))
NN = (((1,), (0,)), ((), ()))
bf16 = jnp.bfloat16
f32 = jnp.float32
VM = pl.BlockSpec(memory_space=pltpu.VMEM)
HBM = pl.BlockSpec(memory_space=pltpu.HBM)
VMEM_LIMIT = 67043328
BLOCK = 128


def snap(value, magic):
    return (value + magic) - magic


def split2(value):
    high = value.astype(bf16)
    return high, (value - high.astype(f32)).astype(bf16)


def rows8(value):
    high, low = split2(value)
    return jnp.concatenate([high.astype(f32), low.astype(f32)], axis=0).astype(bf16)


def fold8(value):
    return value[0:NRHS] + value[NRHS : 2 * NRHS]


def dot2(rows, value, dims):
    high, low = split2(value)
    return lax.dot_general(rows, high, dims, preferred_element_type=f32) + lax.dot_general(
        rows, low, dims, preferred_element_type=f32
    )


def pieces(x0, x1, x2, put):
    n = m = None
    for k, points in enumerate((x0, x1, x2)):
        x = points - 0.5
        h = snap(x, 49152.0)
        low = x - h
        l0 = snap(low, 96.0)
        put(k, h)
        put(8 + k, l0)
        put(11 + k, low - l0)
        n = h * h if n is None else n + h * h
        part = low * (h + h + low)
        m = part if m is None else m + part
    n0 = snap(n, 49152.0)
    m0 = snap(m, 384.0)
    m1 = snap(m - m0, 1.5)
    for row, value in ((3, n0), (4, n - n0), (7, m0), (14, m1), (15, m - m0 - m1)):
        put(row, value)
    one = jnp.ones_like(n)
    put(5, one)
    put(6, one)


def features(points):
    rows = [None] * 16

    def put(row, value):
        rows[row] = value

    pieces(points[0:1], points[1:2], points[2:3], put)
    return jnp.concatenate(rows, axis=0).astype(bf16)


def mixing():
    r = lax.broadcasted_iota(jnp.int32, (16, 64), 0)
    c = lax.broadcasted_iota(jnp.int32, (16, 64), 1)
    h, l0, l1 = (0, 1, 2), (8, 9, 10), (11, 12, 13)
    n0, n1, one, other, m0, m1, m2 = 3, 4, 5, 6, 7, 14, 15
    entries = []
    for k in range(3):
        entries += [(0, h[k], h[k], -2.0)]
        entries += [(1, h[k], l0[k], -2.0), (1, l0[k], h[k], -2.0), (1, l1[k], h[k], -2.0)]
        entries += [(2, h[k], l1[k], -2.0), (2, l0[k], l0[k], -2.0), (2, l1[k], l0[k], -2.0)]
        entries += [(3, l0[k], l1[k], -2.0), (3, l1[k], l1[k], -2.0)]
    entries += [(0, n0, one, 1.0), (0, n1, one, 1.0), (0, one, n0, 1.0), (0, other, n1, 1.0)]
    entries += [(1, m0, one, 1.0), (1, m1, one, 1.0), (1, m2, one, 1.0)]
    entries += [(1, one, m0, 1.0), (1, other, m1, 1.0), (2, one, m2, 1.0)]
    out = jnp.zeros((16, 64), f32)
    for block, source, target, value in entries:
        out = jnp.where((r == target) & (c == 16 * block + source), value, out)
    return out.astype(bf16)


def targets_of(feature_rows, mix):
    return lax.dot_general(feature_rows, mix, TN, preferred_element_type=f32).astype(bf16)


def covariance(squared):
    y = jnp.maximum(squared, TINY)
    return jnp.exp2(y * lax.rsqrt(y) * RATE)


def spread(ref, base, count, feature_rows):
    def put(row, value):
        for q in range(feature_rows.shape[0]):
            feature_rows.at[q][pl.ds(16 * base + row, count, stride=16), :] = value[:, 128 * q : 128 * q + 128]

    pieces(ref[0], ref[1], ref[2], put)


def source_of(slot, feature_rows, source_rows):
    at = pl.ds(pl.multiple_of(16 * slot, 16), 16)
    rows = jnp.concatenate([feature_rows[q, at, :].astype(bf16) for q in range(feature_rows.shape[0])], axis=1)
    for b in range(4):
        source_rows[slot, 16 * b : 16 * b + 16, :] = rows
    return rows


def up_body(
    coords_hbm,
    charges_hbm,
    bases_hbm,
    up_hbm,
    top_hbm,
    copies_hbm,
    beside_hbm,
    across_hbm,
    self_hbm,
    coords,
    charges,
    bases,
    up_transfer,
    top_transfer,
    copies,
    beside,
    across,
    self_part,
    target_rows,
    source_rows,
    source_vals,
    feature_rows,
    square_a,
    square_b,
    kern_a,
    kern_b,
    total_rows,
    sems,
    group_sems,
    *,
    self_unroll,
):
    leaves, _, points = charges.shape
    edge = beside.shape[1]
    group = 4
    mix = mixing()
    small = [
        pltpu.make_async_copy(src, dst, sems.at[k])
        for k, (src, dst) in enumerate(((charges_hbm, charges), (coords_hbm, coords), (top_hbm, top_transfer)))
    ]
    moves = []
    for g in range(leaves // group):
        at = pl.ds(group * g, group)
        moves.append(
            (
                pltpu.make_async_copy(bases_hbm.at[at], bases.at[at], group_sems.at[0, g]),
                pltpu.make_async_copy(up_hbm.at[at], up_transfer.at[at], group_sems.at[1, g]),
            )
        )
    for move in small[0:2] + [m for pair in moves for m in pair] + small[2:]:
        move.start()
    small[0].wait()
    small[1].wait()
    odd = lax.axis_index("leaf") % 2
    sends = []
    for k, (ref, start) in enumerate(((beside, (1 - odd) * (leaves - edge)), (across, odd * (leaves - edge)))):
        start = pl.multiple_of(start, edge)
        for c in range(3):
            ref[c] = coords[c, pl.ds(start, edge), :]
        ref[3] = jnp.zeros(ref.shape[1:], f32)
        for g in range(4):
            ref[4 + g, 0:4, :] = charges[start + 2 * g]
            ref[4 + g, 4:8, :] = charges[start + 2 * g + 1]
        sends.append(pltpu.make_async_copy(ref, (beside_hbm, across_hbm)[k], sems.at[3 + k]))
        sends[k].start()
    spread(coords, 0, leaves, feature_rows)

    def own(i, _):
        target_rows[i] = targets_of(source_of(i, feature_rows, source_rows), mix)
        source_vals[i] = rows8(charges[i])
        return 0

    lax.fori_loop(0, leaves, own, 0, unroll=16)

    def self_distances(t, dst, c):
        rows = slice(c, c + BLOCK)
        dst[rows, c:] = jnp.dot(target_rows[t, rows, :], source_rows[t, :, c:], preferred_element_type=f32)

    def self_kernels(src, dst, c):
        high, low = split2(covariance(src[c : c + BLOCK, c:]))
        dst[0, c : c + BLOCK, c:] = high
        dst[1, c : c + BLOCK, c:] = low

    def self_apply(t, src):
        vals = source_vals[t]
        sums = []
        for c in blocks:
            part = None
            for p in range(2):
                term = lax.dot_general(vals[:, c:], src[p, c : c + BLOCK, c:], NT, preferred_element_type=f32)
                part = term if part is None else part + term
                if c:
                    part += jnp.dot(vals[:, :c], src[p, :c, c : c + BLOCK], preferred_element_type=f32)
            sums.append(part)
        total_rows[t] = jnp.concatenate(sums, axis=1)

    blocks = range(0, points, BLOCK)
    for c in blocks:
        self_distances(0, square_a, c)

    def self_step(k, _):
        i = self_unroll * k
        for u in range(0, self_unroll, 2):
            for c in blocks:
                self_kernels(square_a, kern_a, c)
                self_distances(i + u + 1, square_b, c)
            self_apply(jnp.where(k == 0, leaves, i - 1) if u == 0 else i + u - 1, kern_b)
            for c in blocks:
                self_kernels(square_b, kern_b, c)
                self_distances(i + u + 2, square_a, c)
            self_apply(i + u, kern_a)
        return 0

    lax.fori_loop(0, leaves // self_unroll, self_step, 0)
    self_apply(leaves - 1, kern_b)

    for leaf in range(leaves):
        self_part[leaf] = fold8(total_rows[leaf])
    sends.append(pltpu.make_async_copy(self_part, self_hbm, sems.at[6]))
    sends[2].start()
    for pair in moves:
        for move in pair:
            move.wait()
    small[2].wait()
    coeffs = [rows8(fold8(dot2(source_vals[leaf], bases[leaf], NT))) for leaf in range(leaves)]
    parts = [fold8(dot2(coeffs[leaf], up_transfer[leaf], NT)) for leaf in range(leaves)]
    mids = []
    lift = None
    for n in range(leaves // 8):
        group = parts[8 * n : 8 * n + 8]
        while len(group) > 1:
            group = [a + b for a, b in zip(group[0::2], group[1::2])]
        mids.append(group[0])
        part = fold8(dot2(rows8(group[0]), top_transfer[n], NT))
        lift = part if lift is None else lift + part
    tile = jnp.concatenate(
        [jnp.concatenate(mids, axis=1), jnp.concatenate([lift, jnp.zeros_like(lift)], axis=1)], axis=0
    )
    copies[...] = jnp.broadcast_to(tile, copies.shape)
    sends.append(pltpu.make_async_copy(copies, copies_hbm, sems.at[5]))
    sends[3].start()
    for send in sends:
        send.wait()


def up_call(peers, coords, charges, bases, up_transfer, top_transfer, self_unroll=2):
    leaves, _, points = charges.shape
    halo = (8, EDGE, points)
    copies = (peers, 8, 128)
    args = (coords, charges, bases, up_transfer, top_transfer)
    return pl.pallas_call(
        functools.partial(up_body, self_unroll=self_unroll),
        out_shape=tuple(jax.ShapeDtypeStruct(shape, f32) for shape in (copies, halo, halo, charges.shape)),
        in_specs=[HBM] * 5,
        out_specs=(HBM,) * 4,
        scratch_shapes=[pltpu.VMEM(a.shape, f32) for a in args]
        + [pltpu.VMEM(shape, f32) for shape in (copies, halo, halo, charges.shape)]
        + [
            pltpu.VMEM((leaves + 1, points, 64), bf16),
            pltpu.VMEM((leaves + 1, 64, points), bf16),
            pltpu.VMEM((leaves + 1, 2 * NRHS, points), bf16),
            pltpu.VMEM((points // 128, leaves * 16, 128), f32),
            pltpu.VMEM((points, points), f32),
            pltpu.VMEM((points, points), f32),
            pltpu.VMEM((2, points, points), bf16),
            pltpu.VMEM((2, points, points), bf16),
            pltpu.VMEM((leaves + 1, 2 * NRHS, points), f32),
        ]
        + [pltpu.SemaphoreType.DMA((7,)), pltpu.SemaphoreType.DMA((2, 4))],
        compiler_params=pltpu.CompilerParams(vmem_limit_bytes=VMEM_LIMIT),
        name="upward",
    )(*args)


def near_body(
    list_hbm,
    count_hbm,
    coords_hbm,
    charges_hbm,
    self_hbm,
    beside,
    across,
    out,
    near_list,
    near_count,
    coords,
    charges,
    self_part,
    target_rows,
    source_rows,
    source_vals,
    feature_rows,
    square_a,
    square_b,
    kern_a,
    kern_b,
    total_rows,
    pair_t,
    pair_s,
    sems,
    *,
    chunk,
    unroll,
    own_unroll,
):
    leaves, _, points = charges.shape
    edge = beside.shape[1]
    slots = near_list.shape[0]
    pairs_of = ((coords_hbm, coords), (list_hbm, near_list), (count_hbm, near_count), (charges_hbm, charges))
    pairs_of += ((self_hbm, self_part),)
    moves = [pltpu.make_async_copy(src, dst, sems.at[k]) for k, (src, dst) in enumerate(pairs_of)]
    for move in moves:
        move.start()
    window_start = lax.axis_index("leaf") * leaves - edge
    odd = lax.axis_index("leaf") % 2
    beside_at = (1 - odd) * (edge + leaves)
    across_at = odd * (edge + leaves)
    mix = mixing()
    total_rows[...] = jnp.zeros_like(total_rows)
    for move in moves:
        move.wait()
    total = 0
    for t in range(leaves):
        for j in range(1, slots):
            pair_t[total + j - 1] = t
            pair_s[total + j - 1] = near_list[j, t] - window_start
        total = total + near_count[t] - 1
    for j in range(unroll + 1):
        pair_t[total + j] = leaves
        pair_s[total + j] = 0
    for ref, base, count in ((beside, beside_at, edge), (across, across_at, edge), (coords, edge, leaves)):

        spread(ref, base, count, feature_rows)

    def own(i, _):
        target_rows[i] = targets_of(source_of(edge + i, feature_rows, source_rows), mix)
        source_vals[edge + i] = rows8(charges[i])
        return 0

    lax.fori_loop(0, leaves, own, 0, unroll=own_unroll)

    def halo(g, _):
        for ref, base in ((beside, beside_at), (across, across_at)):
            for k in range(2):
                source_of(base + 2 * g + k, feature_rows, source_rows)
                source_vals[base + 2 * g + k] = rows8(ref[4 + g, 4 * k : 4 * k + 4, :])
        return 0

    lax.fori_loop(0, edge // 2, halo, 0)

    def distances(i, dst, c):
        dst[c : c + chunk, :] = jnp.dot(
            target_rows[pair_t[i], c : c + chunk, :], source_rows[pair_s[i]], preferred_element_type=f32
        )

    def kernels(src, dst, c):
        high, low = split2(covariance(src[c : c + chunk, :]))
        dst[0, c : c + chunk, :] = high
        dst[1, c : c + chunk, :] = low

    def apply(i, src, c):
        vals = source_vals[pair_s[i]]
        total_rows[pair_t[i], :, c : c + chunk] += lax.dot_general(
            vals, src[0, c : c + chunk, :], NT, preferred_element_type=f32
        ) + lax.dot_general(vals, src[1, c : c + chunk, :], NT, preferred_element_type=f32)

    chunks = range(0, points, chunk)
    for c in chunks:
        distances(0, square_a, c)

    def step(k, _):
        i = unroll * k
        previous = jnp.where(k == 0, total, i - 1)
        for u in range(0, unroll, 2):
            for c in chunks:
                kernels(square_a, kern_a, c)
                distances(i + u + 1, square_b, c)
                apply(previous if u == 0 else i + u - 1, kern_b, c)
            for c in chunks:
                kernels(square_b, kern_b, c)
                distances(i + u + 2, square_a, c)
                apply(i + u, kern_a, c)
        return 0

    trips = (total + unroll - 1) // unroll
    lax.fori_loop(0, trips, step, 0)
    for c in chunks:
        apply(jnp.maximum(unroll * trips - 1, 0), kern_b, c)

    def finish(i, _):
        out[i] = fold8(total_rows[i]) + self_part[i]
        return 0

    lax.fori_loop(0, leaves, finish, 0, unroll=4)


def near_call(near_list, near_count, coords, charges, self_part, beside, across, chunk=128, unroll=4, own_unroll=16):
    leaves, _, points = charges.shape
    window = leaves + 2 * EDGE
    pairs = near_list.shape[0] * leaves + unroll + 4
    return pl.pallas_call(
        functools.partial(near_body, chunk=chunk, unroll=unroll, own_unroll=own_unroll),
        out_shape=jax.ShapeDtypeStruct((leaves, NRHS, points), f32),
        in_specs=[HBM] * 5 + [VM] * 2,
        out_specs=VM,
        scratch_shapes=[
            pltpu.SMEM(near_list.shape, jnp.int32),
            pltpu.SMEM(near_count.shape, jnp.int32),
            pltpu.VMEM(coords.shape, f32),
            pltpu.VMEM(charges.shape, f32),
            pltpu.VMEM(charges.shape, f32),
            pltpu.VMEM((leaves + 1, points, 64), bf16),
            pltpu.VMEM((window, 64, points), bf16),
            pltpu.VMEM((window, 2 * NRHS, points), bf16),
            pltpu.VMEM((points // 128, window * 16, 128), f32),
            pltpu.VMEM((points, points), f32),
            pltpu.VMEM((points, points), f32),
            pltpu.VMEM((2, points, points), bf16),
            pltpu.VMEM((2, points, points), bf16),
            pltpu.VMEM((leaves + 1, 2 * NRHS, points), f32),
            pltpu.SMEM((pairs,), jnp.int32),
            pltpu.SMEM((pairs,), jnp.int32),
            pltpu.SemaphoreType.DMA((5,)),
        ],
        compiler_params=pltpu.CompilerParams(vmem_limit_bytes=VMEM_LIMIT),
        name="near",
    )(near_list, near_count, coords, charges, self_part, beside, across)


def far_body(
    far_mid_hbm,
    mid_count_hbm,
    far_top_hbm,
    top_count_hbm,
    proxy_mid_hbm,
    proxy_top_hbm,
    top_hbm,
    up_hbm,
    bases_hbm,
    gathered_hbm,
    near_hbm,
    out,
    far_mid,
    mid_count,
    far_top,
    top_count,
    proxy_mid,
    proxy_top,
    top_transfer,
    up_transfer,
    bases,
    gathered,
    near,
    mid_points,
    top_points,
    pts,
    coef,
    kern,
    sems,
):
    sources = (
        far_mid_hbm,
        mid_count_hbm,
        far_top_hbm,
        top_count_hbm,
        proxy_mid_hbm,
        proxy_top_hbm,
        gathered_hbm,
        top_hbm,
        up_hbm,
        bases_hbm,
        near_hbm,
    )
    inputs = (far_mid, mid_count, far_top, top_count, proxy_mid, proxy_top)
    places = inputs + (gathered, top_transfer, up_transfer, bases, near)
    moves = [pltpu.make_async_copy(src, dst, sems.at[k]) for k, (src, dst) in enumerate(zip(sources, places))]
    for move in moves:
        move.start()
    leaves = near.shape[0]
    nodes = leaves // 8
    rank = bases.shape[1]
    device = lax.axis_index("leaf")
    own = device * nodes
    parent = own // 8
    mix = mixing()
    for move in moves[0:6]:
        move.wait()
    for k in range(3):
        mids, tops = proxy_mid[k].T, proxy_top[k]
        mid_points[pl.ds(k, mids.shape[0], stride=4), :] = jnp.concatenate([mids, mids], axis=1)
        top_points[pl.ds(k, tops.shape[0], stride=4), :] = jnp.concatenate([tops, tops], axis=1)

    def proxy(ref, node):
        return ref[pl.ds(4 * node, 3), :]

    lane = lax.broadcasted_iota(jnp.int32, (NRHS, 2 * rank), 1)

    def kernels_of(k, node, ids, nodes_points):
        slots = ids.shape[0]
        width = rank * slots
        for j in range(0, slots, 2):
            a, b = ids[j, node], ids[j + 1, node]
            pts[k, 0:3, rank * j : rank * j + 2 * rank] = jnp.where(
                lane[0:3] < rank, proxy(nodes_points, a), proxy(nodes_points, b)
            )
        rows = features(pts[k, 0:3, 0:width])
        squared = jnp.dot(
            targets_of(features(proxy(nodes_points, node)[:, 0:rank]), mix),
            jnp.concatenate([rows] * 4, axis=0),
            preferred_element_type=f32,
        )
        high, low = split2(covariance(squared))
        kern[k, 0, :, 0:width] = high
        kern[k, 1, :, 0:width] = low

    def field(k, node, ids, count, coeffs_of):
        slots = ids.shape[0]
        width = rank * slots
        for j in range(0, slots, 2):
            left = jnp.where(j < count, coeffs_of(ids[j, node], 0), 0.0)
            right = jnp.where(j + 1 < count, coeffs_of(ids[j + 1, node], 1), 0.0)
            coef[k, :, rank * j : rank * j + 2 * rank] = jnp.where(lane < rank, left, right)
        vals = rows8(coef[k, :, 0:width])
        return fold8(
            lax.dot_general(vals, kern[k, 0, :, 0:width], NT, preferred_element_type=f32)
            + lax.dot_general(vals, kern[k, 1, :, 0:width], NT, preferred_element_type=f32)
        )

    def mid_coeffs(s, half):
        node = gathered[lax.shift_right_logical(s, 1), 0:NRHS, :]
        return jnp.where((s & 1) == half, node, pltpu.roll(node, rank, 1))

    def top_coeffs(s, half):
        node = gathered[4 * s, NRHS : 2 * NRHS, :]
        for k in range(1, 4):
            node = node + gathered[4 * s + k, NRHS : 2 * NRHS, :]
        return node if half == 0 else pltpu.roll(node, rank, 1)

    kernels_of(nodes, parent, far_top, top_points)
    for n in range(nodes):
        kernels_of(n, own + n, far_mid, mid_points)
    for move in moves[6:]:
        move.wait()
    top8 = rows8(field(nodes, parent, far_top, top_count[parent], top_coeffs))
    mids = []
    for n in range(nodes):
        mid_field = field(n, own + n, far_mid, mid_count[own + n], mid_coeffs)
        mid_field = mid_field + fold8(dot2(top8, top_transfer[n], (((1,), (0,)), ((), ()))))
        mid8 = rows8(mid_field)
        mids.append(mid8)
    fields = [rows8(fold8(dot2(mids[leaf // 8], up_transfer[leaf], NN))) for leaf in range(leaves)]
    for leaf in range(leaves):
        out[leaf] = (near[leaf] + fold8(dot2(fields[leaf], bases[leaf], NN))) * out_scale


def far_call(
    far_mid, mid_count, far_top, top_count, proxy_mid, proxy_top, top_transfer, up_transfer, bases, gathered, near
):
    width = bases.shape[1] * max(far_mid.shape[0], far_top.shape[0])
    integers = (far_mid, mid_count, far_top, top_count)
    floats = (proxy_mid, proxy_top, top_transfer, up_transfer, bases, gathered, near)
    fields = near.shape[0] // 8 + 1
    return pl.pallas_call(
        far_body,
        out_shape=jax.ShapeDtypeStruct(near.shape, f32),
        in_specs=[HBM] * 11,
        out_specs=VM,
        scratch_shapes=[pltpu.SMEM(a.shape, jnp.int32) for a in integers]
        + [pltpu.VMEM(a.shape, f32) for a in floats]
        + [
            pltpu.VMEM((4 * proxy_mid.shape[2], 2 * proxy_mid.shape[1]), f32),
            pltpu.VMEM((4 * proxy_top.shape[1], 2 * proxy_top.shape[2]), f32),
            pltpu.VMEM((fields, 8, width), f32),
            pltpu.VMEM((fields, NRHS, width), f32),
            pltpu.VMEM((fields, 2, bases.shape[1], width), bf16),
            pltpu.SemaphoreType.DMA((11,)),
        ],
        compiler_params=pltpu.CompilerParams(vmem_limit_bytes=VMEM_LIMIT),
        name="far",
    )(*integers, *floats)


def shards(
    coords,
    charges,
    bases,
    up_transfer,
    top_transfer,
    proxy_mid,
    proxy_top,
    near_list,
    near_count,
    far_mid,
    far_mid_count,
    far_top,
    far_top_count,
):
    peers = lax.axis_size("leaf")
    chip = [(i, i ^ 1) for i in range(peers)]
    next_chip = [(i, i + 1 if i % 2 else i - 1) for i in range(1, peers - 1)]
    coords = jnp.transpose(coords, (1, 0, 2))
    copies, beside, across, self_part = up_call(peers, coords, charges, bases, up_transfer, top_transfer)
    across = lax.ppermute(across, "leaf", next_chip)
    beside = lax.ppermute(beside, "leaf", chip)
    gathered = lax.all_to_all(copies, "leaf", 0, 0, tiled=True)
    near = near_call(near_list.T, near_count, coords, charges, self_part, beside, across)
    return far_call(
        far_mid.T,
        far_mid_count,
        far_top.T,
        far_top_count,
        jnp.transpose(proxy_mid, (1, 2, 0)),
        jnp.transpose(proxy_top, (1, 0, 2)),
        top_transfer,
        up_transfer,
        bases,
        gathered,
        near,
    )


def solution(mesh):
    placed = (
        P("leaf", None, None),
        P("leaf", None, None),
        P("leaf", None, None),
        P("leaf", None, None),
        P("leaf", None, None),
        P(),
        P(),
        P("leaf", None),
        P("leaf"),
        P(),
        P(),
        P(),
        P(),
    )
    return jax.shard_map(
        shards, mesh=mesh, in_specs=placed, out_specs=P("leaf", None, None), check_vma=False
    )
```

```python
import functools

import jax
import jax.numpy as jnp
from jax import lax
from jax.experimental import pallas as pl
from jax.experimental.pallas import tpu as pltpu
from jax.sharding import PartitionSpec as P


EDGE = 8
NRHS = 4
length_scale = 0.4
out_scale = 0.125
TINY = 1e-30
RATE = -1.4426950408889634 / length_scale
NT = (((1,), (1,)), ((), ()))
TN = (((0,), (0,)), ((), ()))
NN = (((1,), (0,)), ((), ()))
bf16 = jnp.bfloat16
f32 = jnp.float32
VM = pl.BlockSpec(memory_space=pltpu.VMEM)
HBM = pl.BlockSpec(memory_space=pltpu.HBM)
VMEM_LIMIT = 67043328
BLOCK = 128


def snap(value, magic):
    return (value + magic) - magic


def split2(value):
    high = value.astype(bf16)
    return high, (value - high.astype(f32)).astype(bf16)


def rows8(value):
    high, low = split2(value)
    return jnp.concatenate([high.astype(f32), low.astype(f32)], axis=0).astype(bf16)


def fold8(value):
    return value[0:NRHS] + value[NRHS : 2 * NRHS]


def dot2(rows, value, dims):
    high, low = split2(value)
    return lax.dot_general(rows, high, dims, preferred_element_type=f32) + lax.dot_general(
        rows, low, dims, preferred_element_type=f32
    )


def pieces(x0, x1, x2, put):
    n = m = None
    for k, points in enumerate((x0, x1, x2)):
        x = points - 0.5
        h = snap(x, 49152.0)
        low = x - h
        l0 = snap(low, 96.0)
        put(k, h)
        put(8 + k, l0)
        put(11 + k, low - l0)
        n = h * h if n is None else n + h * h
        part = low * (h + h + low)
        m = part if m is None else m + part
    n0 = snap(n, 49152.0)
    m0 = snap(m, 384.0)
    m1 = snap(m - m0, 1.5)
    for row, value in ((3, n0), (4, n - n0), (7, m0), (14, m1), (15, m - m0 - m1)):
        put(row, value)
    one = jnp.ones_like(n)
    put(5, one)
    put(6, one)


def features(points):
    rows = [None] * 16

    def put(row, value):
        rows[row] = value

    pieces(points[0:1], points[1:2], points[2:3], put)
    return jnp.concatenate(rows, axis=0).astype(bf16)


def mixing():
    r = lax.broadcasted_iota(jnp.int32, (16, 64), 0)
    c = lax.broadcasted_iota(jnp.int32, (16, 64), 1)
    h, l0, l1 = (0, 1, 2), (8, 9, 10), (11, 12, 13)
    n0, n1, one, other, m0, m1, m2 = 3, 4, 5, 6, 7, 14, 15
    entries = []
    for k in range(3):
        entries += [(0, h[k], h[k], -2.0)]
        entries += [(1, h[k], l0[k], -2.0), (1, l0[k], h[k], -2.0), (1, l1[k], h[k], -2.0)]
        entries += [(2, h[k], l1[k], -2.0), (2, l0[k], l0[k], -2.0), (2, l1[k], l0[k], -2.0)]
        entries += [(3, l0[k], l1[k], -2.0), (3, l1[k], l1[k], -2.0)]
    entries += [(0, n0, one, 1.0), (0, n1, one, 1.0), (0, one, n0, 1.0), (0, other, n1, 1.0)]
    entries += [(1, m0, one, 1.0), (1, m1, one, 1.0), (1, m2, one, 1.0)]
    entries += [(1, one, m0, 1.0), (1, other, m1, 1.0), (2, one, m2, 1.0)]
    out = jnp.zeros((16, 64), f32)
    for block, source, target, value in entries:
        out = jnp.where((r == target) & (c == 16 * block + source), value, out)
    return out.astype(bf16)


def targets_of(feature_rows, mix):
    return lax.dot_general(feature_rows, mix, TN, preferred_element_type=f32).astype(bf16)


def covariance(squared):
    y = jnp.maximum(squared, TINY)
    return jnp.exp2(y * lax.rsqrt(y) * RATE)


def spread(ref, base, count, feature_rows):
    def put(row, value):
        for q in range(feature_rows.shape[0]):
            feature_rows.at[q][pl.ds(16 * base + row, count, stride=16), :] = value[:, 128 * q : 128 * q + 128]

    pieces(ref[0], ref[1], ref[2], put)


def source_of(slot, feature_rows, source_rows):
    at = pl.ds(pl.multiple_of(16 * slot, 16), 16)
    rows = jnp.concatenate([feature_rows[q, at, :].astype(bf16) for q in range(feature_rows.shape[0])], axis=1)
    for b in range(4):
        source_rows[slot, 16 * b : 16 * b + 16, :] = rows
    return rows


def up_body(
    coords_hbm,
    charges_hbm,
    bases_hbm,
    up_hbm,
    top_hbm,
    copies_hbm,
    beside_hbm,
    across_hbm,
    self_hbm,
    coords,
    charges,
    bases,
    up_transfer,
    top_transfer,
    copies,
    beside,
    across,
    self_part,
    target_rows,
    source_rows,
    source_vals,
    feature_rows,
    square_a,
    square_b,
    kern_a,
    kern_b,
    total_rows,
    sems,
    group_sems,
    *,
    self_unroll,
):
    leaves, _, points = charges.shape
    edge = beside.shape[1]
    group = 4
    mix = mixing()
    small = [
        pltpu.make_async_copy(src, dst, sems.at[k])
        for k, (src, dst) in enumerate(((charges_hbm, charges), (coords_hbm, coords), (top_hbm, top_transfer)))
    ]
    moves = []
    for g in range(leaves // group):
        at = pl.ds(group * g, group)
        moves.append(
            (
                pltpu.make_async_copy(bases_hbm.at[at], bases.at[at], group_sems.at[0, g]),
                pltpu.make_async_copy(up_hbm.at[at], up_transfer.at[at], group_sems.at[1, g]),
            )
        )
    for move in small[0:2] + [m for pair in moves for m in pair] + small[2:]:
        move.start()
    small[0].wait()
    small[1].wait()
    odd = lax.axis_index("leaf") % 2
    sends = []
    for k, (ref, start) in enumerate(((beside, (1 - odd) * (leaves - edge)), (across, odd * (leaves - edge)))):
        start = pl.multiple_of(start, edge)
        for c in range(3):
            ref[c] = coords[c, pl.ds(start, edge), :]
        ref[3] = jnp.zeros(ref.shape[1:], f32)
        for g in range(4):
            ref[4 + g, 0:4, :] = charges[start + 2 * g]
            ref[4 + g, 4:8, :] = charges[start + 2 * g + 1]
        sends.append(pltpu.make_async_copy(ref, (beside_hbm, across_hbm)[k], sems.at[3 + k]))
        sends[k].start()
    spread(coords, 0, leaves, feature_rows)

    def own(i, _):
        target_rows[i] = targets_of(source_of(i, feature_rows, source_rows), mix)
        source_vals[i] = rows8(charges[i])
        return 0

    lax.fori_loop(0, leaves, own, 0, unroll=16)

    def self_distances(t, dst, c):
        rows = slice(c, c + BLOCK)
        dst[rows, c:] = jnp.dot(target_rows[t, rows, :], source_rows[t, :, c:], preferred_element_type=f32)

    def self_kernels(src, dst, c):
        high, low = split2(covariance(src[c : c + BLOCK, c:]))
        dst[0, c : c + BLOCK, c:] = high
        dst[1, c : c + BLOCK, c:] = low

    def self_apply(t, src):
        vals = source_vals[t]
        sums = []
        for c in blocks:
            part = None
            for p in range(2):
                term = lax.dot_general(vals[:, c:], src[p, c : c + BLOCK, c:], NT, preferred_element_type=f32)
                part = term if part is None else part + term
                if c:
                    part += jnp.dot(vals[:, :c], src[p, :c, c : c + BLOCK], preferred_element_type=f32)
            sums.append(part)
        total_rows[t] = jnp.concatenate(sums, axis=1)

    blocks = range(0, points, BLOCK)
    for c in blocks:
        self_distances(0, square_a, c)

    def self_step(k, _):
        i = self_unroll * k
        for u in range(0, self_unroll, 2):
            for c in blocks:
                self_kernels(square_a, kern_a, c)
                self_distances(i + u + 1, square_b, c)
            self_apply(jnp.where(k == 0, leaves, i - 1) if u == 0 else i + u - 1, kern_b)
            for c in blocks:
                self_kernels(square_b, kern_b, c)
                self_distances(i + u + 2, square_a, c)
            self_apply(i + u, kern_a)
        return 0

    lax.fori_loop(0, leaves // self_unroll, self_step, 0)
    self_apply(leaves - 1, kern_b)

    for leaf in range(leaves):
        self_part[leaf] = fold8(total_rows[leaf])
    sends.append(pltpu.make_async_copy(self_part, self_hbm, sems.at[6]))
    sends[2].start()
    for pair in moves:
        for move in pair:
            move.wait()
    small[2].wait()
    coeffs = [rows8(fold8(dot2(source_vals[leaf], bases[leaf], NT))) for leaf in range(leaves)]
    parts = [fold8(dot2(coeffs[leaf], up_transfer[leaf], NT)) for leaf in range(leaves)]
    mids = []
    lift = None
    for n in range(leaves // 8):
        group = parts[8 * n : 8 * n + 8]
        while len(group) > 1:
            group = [a + b for a, b in zip(group[0::2], group[1::2])]
        mids.append(group[0])
        part = fold8(dot2(rows8(group[0]), top_transfer[n], NT))
        lift = part if lift is None else lift + part
    tile = jnp.concatenate(
        [jnp.concatenate(mids, axis=1), jnp.concatenate([lift, jnp.zeros_like(lift)], axis=1)], axis=0
    )
    copies[...] = jnp.broadcast_to(tile, copies.shape)
    sends.append(pltpu.make_async_copy(copies, copies_hbm, sems.at[5]))
    sends[3].start()
    for send in sends:
        send.wait()


def up_call(peers, coords, charges, bases, up_transfer, top_transfer, self_unroll=2):
    leaves, _, points = charges.shape
    halo = (8, EDGE, points)
    copies = (peers, 8, 128)
    args = (coords, charges, bases, up_transfer, top_transfer)
    return pl.pallas_call(
        functools.partial(up_body, self_unroll=self_unroll),
        out_shape=tuple(jax.ShapeDtypeStruct(shape, f32) for shape in (copies, halo, halo, charges.shape)),
        in_specs=[HBM] * 5,
        out_specs=(HBM,) * 4,
        scratch_shapes=[pltpu.VMEM(a.shape, f32) for a in args]
        + [pltpu.VMEM(shape, f32) for shape in (copies, halo, halo, charges.shape)]
        + [
            pltpu.VMEM((leaves + 1, points, 64), bf16),
            pltpu.VMEM((leaves + 1, 64, points), bf16),
            pltpu.VMEM((leaves + 1, 2 * NRHS, points), bf16),
            pltpu.VMEM((points // 128, leaves * 16, 128), f32),
            pltpu.VMEM((points, points), f32),
            pltpu.VMEM((points, points), f32),
            pltpu.VMEM((2, points, points), bf16),
            pltpu.VMEM((2, points, points), bf16),
            pltpu.VMEM((leaves + 1, 2 * NRHS, points), f32),
        ]
        + [pltpu.SemaphoreType.DMA((7,)), pltpu.SemaphoreType.DMA((2, 4))],
        compiler_params=pltpu.CompilerParams(vmem_limit_bytes=VMEM_LIMIT),
        name="upward",
    )(*args)


def near_body(
    list_hbm,
    count_hbm,
    coords_hbm,
    charges_hbm,
    self_hbm,
    beside,
    across,
    out,
    near_list,
    near_count,
    coords,
    charges,
    self_part,
    target_rows,
    source_rows,
    source_vals,
    feature_rows,
    square_a,
    square_b,
    kern_a,
    kern_b,
    total_rows,
    pair_t,
    pair_s,
    sems,
    *,
    chunk,
    unroll,
    own_unroll,
):
    leaves, _, points = charges.shape
    edge = beside.shape[1]
    slots = near_list.shape[0]
    pairs_of = ((coords_hbm, coords), (list_hbm, near_list), (count_hbm, near_count), (charges_hbm, charges))
    pairs_of += ((self_hbm, self_part),)
    moves = [pltpu.make_async_copy(src, dst, sems.at[k]) for k, (src, dst) in enumerate(pairs_of)]
    for move in moves:
        move.start()
    window_start = lax.axis_index("leaf") * leaves - edge
    odd = lax.axis_index("leaf") % 2
    beside_at = (1 - odd) * (edge + leaves)
    across_at = odd * (edge + leaves)
    mix = mixing()
    total_rows[...] = jnp.zeros_like(total_rows)
    for move in moves:
        move.wait()
    total = 0
    for t in range(leaves):
        for j in range(1, slots):
            pair_t[total + j - 1] = t
            pair_s[total + j - 1] = near_list[j, t] - window_start
        total = total + near_count[t] - 1
    for j in range(unroll + 1):
        pair_t[total + j] = leaves
        pair_s[total + j] = 0
    for ref, base, count in ((beside, beside_at, edge), (across, across_at, edge), (coords, edge, leaves)):

        spread(ref, base, count, feature_rows)

    def own(i, _):
        target_rows[i] = targets_of(source_of(edge + i, feature_rows, source_rows), mix)
        source_vals[edge + i] = rows8(charges[i])
        return 0

    lax.fori_loop(0, leaves, own, 0, unroll=own_unroll)

    def halo(g, _):
        for ref, base in ((beside, beside_at), (across, across_at)):
            for k in range(2):
                source_of(base + 2 * g + k, feature_rows, source_rows)
                source_vals[base + 2 * g + k] = rows8(ref[4 + g, 4 * k : 4 * k + 4, :])
        return 0

    lax.fori_loop(0, edge // 2, halo, 0)

    def distances(i, dst, c):
        dst[c : c + chunk, :] = jnp.dot(
            target_rows[pair_t[i], c : c + chunk, :], source_rows[pair_s[i]], preferred_element_type=f32
        )

    def kernels(src, dst, c):
        high, low = split2(covariance(src[c : c + chunk, :]))
        dst[0, c : c + chunk, :] = high
        dst[1, c : c + chunk, :] = low

    def apply(i, src, c):
        vals = source_vals[pair_s[i]]
        total_rows[pair_t[i], :, c : c + chunk] += lax.dot_general(
            vals, src[0, c : c + chunk, :], NT, preferred_element_type=f32
        ) + lax.dot_general(vals, src[1, c : c + chunk, :], NT, preferred_element_type=f32)

    chunks = range(0, points, chunk)
    for c in chunks:
        distances(0, square_a, c)

    def step(k, _):
        i = unroll * k
        previous = jnp.where(k == 0, total, i - 1)
        for u in range(0, unroll, 2):
            for c in chunks:
                kernels(square_a, kern_a, c)
                distances(i + u + 1, square_b, c)
                apply(previous if u == 0 else i + u - 1, kern_b, c)
            for c in chunks:
                kernels(square_b, kern_b, c)
                distances(i + u + 2, square_a, c)
                apply(i + u, kern_a, c)
        return 0

    trips = (total + unroll - 1) // unroll
    lax.fori_loop(0, trips, step, 0)
    for c in chunks:
        apply(jnp.maximum(unroll * trips - 1, 0), kern_b, c)

    def finish(i, _):
        out[i] = fold8(total_rows[i]) + self_part[i]
        return 0

    lax.fori_loop(0, leaves, finish, 0, unroll=4)


def near_call(near_list, near_count, coords, charges, self_part, beside, across, chunk=128, unroll=4, own_unroll=16):
    leaves, _, points = charges.shape
    window = leaves + 2 * EDGE
    pairs = near_list.shape[0] * leaves + unroll + 4
    return pl.pallas_call(
        functools.partial(near_body, chunk=chunk, unroll=unroll, own_unroll=own_unroll),
        out_shape=jax.ShapeDtypeStruct((leaves, NRHS, points), f32),
        in_specs=[HBM] * 5 + [VM] * 2,
        out_specs=VM,
        scratch_shapes=[
            pltpu.SMEM(near_list.shape, jnp.int32),
            pltpu.SMEM(near_count.shape, jnp.int32),
            pltpu.VMEM(coords.shape, f32),
            pltpu.VMEM(charges.shape, f32),
            pltpu.VMEM(charges.shape, f32),
            pltpu.VMEM((leaves + 1, points, 64), bf16),
            pltpu.VMEM((window, 64, points), bf16),
            pltpu.VMEM((window, 2 * NRHS, points), bf16),
            pltpu.VMEM((points // 128, window * 16, 128), f32),
            pltpu.VMEM((points, points), f32),
            pltpu.VMEM((points, points), f32),
            pltpu.VMEM((2, points, points), bf16),
            pltpu.VMEM((2, points, points), bf16),
            pltpu.VMEM((leaves + 1, 2 * NRHS, points), f32),
            pltpu.SMEM((pairs,), jnp.int32),
            pltpu.SMEM((pairs,), jnp.int32),
            pltpu.SemaphoreType.DMA((5,)),
        ],
        compiler_params=pltpu.CompilerParams(vmem_limit_bytes=VMEM_LIMIT),
        name="near",
    )(near_list, near_count, coords, charges, self_part, beside, across)


def far_body(
    far_mid_hbm,
    mid_count_hbm,
    far_top_hbm,
    top_count_hbm,
    proxy_mid_hbm,
    proxy_top_hbm,
    top_hbm,
    up_hbm,
    bases_hbm,
    gathered_hbm,
    near_hbm,
    out,
    far_mid,
    mid_count,
    far_top,
    top_count,
    proxy_mid,
    proxy_top,
    top_transfer,
    up_transfer,
    bases,
    gathered,
    near,
    mid_points,
    top_points,
    pts,
    coef,
    kern,
    sems,
):
    sources = (
        far_mid_hbm,
        mid_count_hbm,
        far_top_hbm,
        top_count_hbm,
        proxy_mid_hbm,
        proxy_top_hbm,
        gathered_hbm,
        top_hbm,
        up_hbm,
        bases_hbm,
        near_hbm,
    )
    inputs = (far_mid, mid_count, far_top, top_count, proxy_mid, proxy_top)
    places = inputs + (gathered, top_transfer, up_transfer, bases, near)
    moves = [pltpu.make_async_copy(src, dst, sems.at[k]) for k, (src, dst) in enumerate(zip(sources, places))]
    for move in moves:
        move.start()
    leaves = near.shape[0]
    nodes = leaves // 8
    rank = bases.shape[1]
    device = lax.axis_index("leaf")
    own = device * nodes
    parent = own // 8
    mix = mixing()
    for move in moves[0:6]:
        move.wait()
    for k in range(3):
        mids, tops = proxy_mid[k].T, proxy_top[k]
        mid_points[pl.ds(k, mids.shape[0], stride=4), :] = jnp.concatenate([mids, mids], axis=1)
        top_points[pl.ds(k, tops.shape[0], stride=4), :] = jnp.concatenate([tops, tops], axis=1)

    def proxy(ref, node):
        return ref[pl.ds(4 * node, 3), :]

    lane = lax.broadcasted_iota(jnp.int32, (NRHS, 2 * rank), 1)

    def kernels_of(k, node, ids, nodes_points):
        slots = ids.shape[0]
        width = rank * slots
        for j in range(0, slots, 2):
            a, b = ids[j, node], ids[j + 1, node]
            pts[k, 0:3, rank * j : rank * j + 2 * rank] = jnp.where(
                lane[0:3] < rank, proxy(nodes_points, a), proxy(nodes_points, b)
            )
        rows = features(pts[k, 0:3, 0:width])
        squared = jnp.dot(
            targets_of(features(proxy(nodes_points, node)[:, 0:rank]), mix),
            jnp.concatenate([rows] * 4, axis=0),
            preferred_element_type=f32,
        )
        high, low = split2(covariance(squared))
        kern[k, 0, :, 0:width] = high
        kern[k, 1, :, 0:width] = low

    def field(k, node, ids, count, coeffs_of):
        slots = ids.shape[0]
        width = rank * slots
        for j in range(0, slots, 2):
            left = jnp.where(j < count, coeffs_of(ids[j, node], 0), 0.0)
            right = jnp.where(j + 1 < count, coeffs_of(ids[j + 1, node], 1), 0.0)
            coef[k, :, rank * j : rank * j + 2 * rank] = jnp.where(lane < rank, left, right)
        vals = rows8(coef[k, :, 0:width])
        return fold8(
            lax.dot_general(vals, kern[k, 0, :, 0:width], NT, preferred_element_type=f32)
            + lax.dot_general(vals, kern[k, 1, :, 0:width], NT, preferred_element_type=f32)
        )

    def mid_coeffs(s, half):
        node = gathered[lax.shift_right_logical(s, 1), 0:NRHS, :]
        return jnp.where((s & 1) == half, node, pltpu.roll(node, rank, 1))

    def top_coeffs(s, half):
        node = gathered[4 * s, NRHS : 2 * NRHS, :]
        for k in range(1, 4):
            node = node + gathered[4 * s + k, NRHS : 2 * NRHS, :]
        return node if half == 0 else pltpu.roll(node, rank, 1)

    kernels_of(nodes, parent, far_top, top_points)
    for n in range(nodes):
        kernels_of(n, own + n, far_mid, mid_points)
    moves[6].wait()
    top8 = rows8(field(nodes, parent, far_top, top_count[parent], top_coeffs))
    sums = [field(n, own + n, far_mid, mid_count[own + n], mid_coeffs) for n in range(nodes)]
    moves[7].wait()
    moves[8].wait()
    mids = [rows8(sums[n] + fold8(dot2(top8, top_transfer[n], NN))) for n in range(nodes)]
    fields = [rows8(fold8(dot2(mids[leaf // 8], up_transfer[leaf], NN))) for leaf in range(leaves)]
    moves[9].wait()
    moves[10].wait()
    for leaf in range(leaves):
        out[leaf] = (near[leaf] + fold8(dot2(fields[leaf], bases[leaf], NN))) * out_scale


def far_call(
    far_mid, mid_count, far_top, top_count, proxy_mid, proxy_top, top_transfer, up_transfer, bases, gathered, near
):
    width = bases.shape[1] * max(far_mid.shape[0], far_top.shape[0])
    integers = (far_mid, mid_count, far_top, top_count)
    floats = (proxy_mid, proxy_top, top_transfer, up_transfer, bases, gathered, near)
    fields = near.shape[0] // 8 + 1
    return pl.pallas_call(
        far_body,
        out_shape=jax.ShapeDtypeStruct(near.shape, f32),
        in_specs=[HBM] * 11,
        out_specs=VM,
        scratch_shapes=[pltpu.SMEM(a.shape, jnp.int32) for a in integers]
        + [pltpu.VMEM(a.shape, f32) for a in floats]
        + [
            pltpu.VMEM((4 * proxy_mid.shape[2], 2 * proxy_mid.shape[1]), f32),
            pltpu.VMEM((4 * proxy_top.shape[1], 2 * proxy_top.shape[2]), f32),
            pltpu.VMEM((fields, 8, width), f32),
            pltpu.VMEM((fields, NRHS, width), f32),
            pltpu.VMEM((fields, 2, bases.shape[1], width), bf16),
            pltpu.SemaphoreType.DMA((11,)),
        ],
        compiler_params=pltpu.CompilerParams(vmem_limit_bytes=VMEM_LIMIT),
        name="far",
    )(*integers, *floats)


def shards(
    coords,
    charges,
    bases,
    up_transfer,
    top_transfer,
    proxy_mid,
    proxy_top,
    near_list,
    near_count,
    far_mid,
    far_mid_count,
    far_top,
    far_top_count,
):
    peers = lax.axis_size("leaf")
    chip = [(i, i ^ 1) for i in range(peers)]
    next_chip = [(i, i + 1 if i % 2 else i - 1) for i in range(1, peers - 1)]
    coords = jnp.transpose(coords, (1, 0, 2))
    copies, beside, across, self_part = up_call(peers, coords, charges, bases, up_transfer, top_transfer)
    across = lax.ppermute(across, "leaf", next_chip)
    beside = lax.ppermute(beside, "leaf", chip)
    gathered = lax.all_to_all(copies, "leaf", 0, 0, tiled=True)
    near = near_call(near_list.T, near_count, coords, charges, self_part, beside, across)
    return far_call(
        far_mid.T,
        far_mid_count,
        far_top.T,
        far_top_count,
        jnp.transpose(proxy_mid, (1, 2, 0)),
        jnp.transpose(proxy_top, (1, 0, 2)),
        top_transfer,
        up_transfer,
        bases,
        gathered,
        near,
    )


def solution(mesh):
    placed = (
        P("leaf", None, None),
        P("leaf", None, None),
        P("leaf", None, None),
        P("leaf", None, None),
        P("leaf", None, None),
        P(),
        P(),
        P("leaf", None),
        P("leaf"),
        P(),
        P(),
        P(),
        P(),
    )
    return jax.shard_map(
        shards, mesh=mesh, in_specs=placed, out_specs=P("leaf", None, None), check_vma=False
    )
```
